256 devices in a mesh: dp: 64 (over z, x, core), rep: 4 (over y).
Axes of the slice: x: 4, y: 4, z: 8, core: 2. Of those that a mesh axis runs over, the one named last changes fastest.
Arguments:
- ecg: bfloat16 [4, 327680], P('rep', 'dp'), may hold values from -6 to 6
- conv_first: bfloat16 [5, 256], replicated, may hold values from -2.5 to 2.5
- conv_second: bfloat16 [512, 256], replicated, may hold values from -0.25 to 0.25
- conv_third: bfloat16 [512, 256], replicated, may hold values from -0.25 to 0.25
- enc_gain: float32 [256], replicated, may hold values from 0.1 to 1.9
- ctx_weight: bfloat16 [2, 512, 256], replicated, may hold values from -0.25 to 0.25
- head_weight: bfloat16 [256, 12, 256], replicated, may hold values from -0.375 to 0.375
- sources: int32 [4, 512, 4, 2], P('rep', 'dp'), may hold values from 0 to 63, as said below
Outputs:
- target_grad: float32 [4, 16384, 256], P('rep', 'dp')
- head_grad: float32 [4, 256, 12, 256], P('rep')
The draws below stay inside these ranges and needn't reach their ends.
Inputs may be any that keep to these rules, and one draw needn't show every extreme that they name: sources[r, i, s] = (o, b): o is the piece index along the recording, b a block of 128 rows of that piece's 256 positions. Among the 32 entries of one piece at most 2 name the same piece o, and in every draw one piece o is named exactly 2 times by every piece of its recording.
All inputs are finite; a program needn't handle non-finite values.
Results may differ from the reference program's by a relative error of at most 0.0085.
Values may be sent and summed in bfloat16 or wider, within the bound.
No kernel may reach another device: no remote copies, remote signals or barrier semaphores. Data moves between devices by JAX's collectives and lax.ppermute only.
A program may use at most 128 MiB of HBM per device.

```python
import math
import jax
import jax.numpy as jnp
from jax import lax

C = 256
K = 12
LAYERS = 2
NEGB = 4
TZ = 256
QG = 8
NB = 32
CAP = 2
SAMP_DEV = 5120
SAMPLES = 327680
RECS = 4
N_DP = 64


def draw_sources(key, part):
    record_keys = jax.random.split(jax.random.fold_in(key, 11), RECS)

    def draw_record(record_key):
        busy_owner = jax.random.randint(jax.random.fold_in(record_key, 1), (), 0, N_DP, dtype=jnp.int32)
        device_keys = jax.random.split(jax.random.fold_in(record_key, 2), N_DP)

        def draw_device(device_key):
            key_order = jax.random.fold_in(device_key, 3)
            key_shuffle = jax.random.fold_in(device_key, 4)
            key_blocks = jax.random.fold_in(device_key, 5)
            owner_pool = jnp.tile(jnp.arange(N_DP, dtype=jnp.int32), CAP)
            priority = jax.random.permutation(key_order, N_DP * CAP).astype(jnp.int32)
            priority = jnp.where(owner_pool == busy_owner, priority - N_DP * CAP, priority)
            ranking = jnp.argsort(priority, stable=True)
            owners = owner_pool[ranking[:NB]]
            owners = owners[jax.random.permutation(key_shuffle, NB)]
            blocks = jax.random.randint(key_blocks, (NB,), 0, TZ // 128, dtype=jnp.int32)
            return jnp.stack([owners, blocks], -1).reshape(QG, NEGB, 2)
        return jax.vmap(draw_device)(device_keys).reshape(N_DP * QG, NEGB, 2)
    return jax.vmap(draw_record)(record_keys).astype(jnp.int32)


def shard_levels(stream_key, shape, cuts, low, top_value):
    def one(dim, parts):
        heights = jax.random.uniform(jax.random.fold_in(jax.random.fold_in(stream_key, 6), dim), (parts,), jnp.float32, low / len(cuts), top_value / len(cuts))
        return jnp.repeat(jnp.exp(heights), shape[dim] // parts).reshape((-1,) + (1,) * (len(shape) - dim - 1))

    loudness = one(*cuts[0])
    for cut in cuts[1:]:
        loudness = loudness * one(*cut)
    return loudness


def noise(rng, extent, scale, limit, shards=(), kind=jnp.bfloat16):
    factor_of = shard_levels(rng, extent, shards, -0.22, 0.18) if shards else 1.0
    values = jax.random.normal(rng, extent, jnp.float32) * scale * factor_of
    return jnp.minimum(jnp.maximum(values, -limit), limit).astype(kind)


def setup_inputs(seed: int = 0) -> dict:
    keys = jax.random.split(jax.random.key(seed), 9)
    ecg = noise(keys[0], (RECS, SAMPLES), 1.0, 6.0, ((0, 4), (1, 64)))
    conv_first = noise(keys[1], (5, C), 5 ** -0.5, 2.5)
    conv_second = noise(keys[2], (2 * C, C), (2 * C) ** -0.5, 0.25)
    conv_third = noise(keys[3], (2 * C, C), (2 * C) ** -0.5, 0.25)
    enc_gain = jnp.clip(1.0 + 0.18 * jax.random.normal(keys[4], (C,), jnp.float32), 0.1, 1.9)
    ctx_weight = noise(keys[5], (LAYERS, 2 * C, C), (2 * C) ** -0.5, 0.25)
    head_weight = noise(keys[6], (C, K, C), C ** -0.5, 0.375)
    sources = draw_sources(jax.random.fold_in(keys[8], 71), 0)
    return dict(ecg=ecg, conv_first=conv_first, conv_second=conv_second, conv_third=conv_third, enc_gain=enc_gain, ctx_weight=ctx_weight, head_weight=head_weight, sources=sources)


def gelu_exact(values):
    return jax.nn.gelu(values, approximate=False)

def encode(piece, conv_first, conv_second, conv_third, enc_gain, ctx_weight):
    channels = conv_first.shape[1]
    positions = piece.shape[0] // 20
    frames = piece.reshape(4 * positions, 5)
    hidden_one = gelu_exact(jnp.dot(frames, conv_first, preferred_element_type=jnp.float32)).astype(jnp.bfloat16)
    hidden_two = gelu_exact(jnp.dot(hidden_one.reshape(2 * positions, 2 * channels), conv_second, preferred_element_type=jnp.float32)).astype(jnp.bfloat16)
    mixed = jnp.dot(hidden_two.reshape(positions, 2 * channels), conv_third, preferred_element_type=jnp.float32)
    average = lax.optimization_barrier(jnp.mean(mixed, -1, keepdims=True))
    centred = mixed - average
    variance = lax.optimization_barrier(jnp.mean(centred * centred, -1, keepdims=True))
    latent = (centred / jnp.sqrt(variance + 1e-05) * enc_gain).astype(jnp.bfloat16)
    latent_wide = latent.astype(jnp.float32)
    target = (latent_wide / jnp.sqrt(lax.optimization_barrier(jnp.sum(latent_wide * latent_wide, -1, keepdims=True)) + 1e-06)).astype(jnp.bfloat16)
    context = latent
    for layer_index in range(ctx_weight.shape[0]):
        dilation = 2 ** layer_index
        before = jnp.concatenate([jnp.zeros((dilation, channels), jnp.bfloat16), context[:positions - dilation]], 0)
        joined = jnp.concatenate([context, before], 1)
        update = gelu_exact(jnp.dot(joined, ctx_weight[layer_index], preferred_element_type=jnp.float32))
        context = (context.astype(jnp.float32) + update).astype(jnp.bfloat16)
    return (target, context)

def score_piece(target, context, head_weight, negatives):
    positions, channels = target.shape
    horizon = head_weight.shape[1]
    groups = negatives.shape[0]
    pred = jnp.dot(context, head_weight.reshape(channels, horizon * channels), preferred_element_type=jnp.float32).reshape(positions, horizon, channels)
    pred_norm = jnp.sqrt(lax.optimization_barrier(jnp.sum(pred * pred, -1, keepdims=True)) + 1e-06)
    unit_pred = pred / pred_norm
    queries = unit_pred.astype(jnp.bfloat16)
    shifted = jnp.stack([jnp.concatenate([target[step_index + 1:], jnp.zeros((step_index + 1, channels), jnp.bfloat16)], 0) for step_index in range(horizon)], 1)
    usable = (lax.broadcasted_iota(jnp.int32, (positions, horizon), 0) + lax.broadcasted_iota(jnp.int32, (positions, horizon), 1) + 1 < positions).astype(jnp.float32)
    positive = 10.0 * lax.optimization_barrier(jnp.sum(queries.astype(jnp.float32) * shifted.astype(jnp.float32), -1))
    grouped = queries.reshape(groups, -1, channels)
    negative = 10.0 * jnp.einsum('gqc,gnc->gqn', grouped.astype(jnp.float32), negatives.astype(jnp.float32))
    pos_exp = jnp.exp(positive)
    neg_exp = jnp.exp(negative)
    partition = pos_exp.reshape(groups, -1) + lax.optimization_barrier(jnp.sum(neg_exp, -1))
    usable_grouped = usable.reshape(groups, -1)
    pos_weight = 10.0 * usable * (pos_exp / partition.reshape(positions, horizon) - 1.0)
    neg_weight = (10.0 * usable_grouped[:, :, None] * neg_exp / partition[:, :, None]).astype(jnp.bfloat16)
    neg_part = jnp.einsum('gqn,gnc->gqc', neg_weight.astype(jnp.float32), negatives.astype(jnp.float32))
    query_grad = pos_weight[:, :, None] * shifted.astype(jnp.float32) + neg_part.reshape(positions, horizon, channels)
    neg_grad = jnp.einsum('gqn,gqc->gnc', neg_weight.astype(jnp.float32), grouped.astype(jnp.float32)).astype(jnp.bfloat16)
    pos_terms = pos_weight[:, :, None] * queries.astype(jnp.float32)
    pos_grad = jnp.zeros((positions, channels), jnp.float32)
    for step_index in range(horizon):
        moved = jnp.concatenate([jnp.zeros((step_index + 1, channels), jnp.float32), pos_terms[:positions - step_index - 1, step_index]], 0)
        pos_grad = pos_grad + moved
    radial = lax.optimization_barrier(jnp.sum(unit_pred * query_grad, -1, keepdims=True))
    pred_grad = ((query_grad - unit_pred * radial) / pred_norm).astype(jnp.bfloat16).reshape(positions, horizon * channels)
    head_part = jnp.dot(context.T, pred_grad, preferred_element_type=jnp.float32)
    return (pos_grad, neg_grad, head_part)

def reference(ecg, conv_first, conv_second, conv_third, enc_gain, ctx_weight, head_weight, sources):
    pieces = ecg.reshape(RECS * N_DP, SAMP_DEV)

    def encode_piece(piece):
        return encode(piece, conv_first, conv_second, conv_third, enc_gain, ctx_weight)
    targets, contexts = lax.map(encode_piece, pieces)
    target_bank = targets.reshape(RECS, N_DP * TZ, C)
    source_rows = sources.reshape(RECS * N_DP, NB, 2)
    offsets = jnp.arange(128, dtype=jnp.int32)

    def visit(current, element):
        target, context, entries, position = element
        record = (position // N_DP).astype(jnp.int32)
        record_bank = lax.dynamic_index_in_dim(target_bank, record, 0, keepdims=False)
        wanted = (entries[:, 0] * TZ + entries[:, 1] * 128).astype(jnp.int32)[:, None] + offsets[None, :]
        negatives = jnp.take(record_bank, wanted.reshape(-1), axis=0).reshape(QG, NEGB * 128, C)
        pos_grad, neg_grad, head_part = score_piece(target, context, head_weight, negatives)
        return (current.at[record].add(head_part), (pos_grad, neg_grad))
    start_sum = jnp.zeros((RECS, C, K * C), jnp.float32)
    head_total, (pos_grads, neg_grads) = lax.scan(visit, start_sum, (targets, contexts, source_rows, jnp.arange(RECS * N_DP, dtype=jnp.int32)))
    record_of = (jnp.arange(RECS * N_DP, dtype=jnp.int32) // N_DP).astype(jnp.int32)
    global_rows = (record_of[:, None] * (N_DP * TZ) + source_rows[:, :, 0] * TZ + source_rows[:, :, 1] * 128).astype(jnp.int32)[:, :, None] + offsets[None, None, :]
    flat_grad = pos_grads.reshape(RECS * N_DP * TZ, C)
    flat_grad = flat_grad.at[global_rows.reshape(-1)].add(neg_grads.reshape(-1, C).astype(jnp.float32))
    target_grad = (flat_grad / K).reshape(RECS, N_DP * TZ, C)
    factor = math.sqrt(C / (N_DP * TZ))
    head_grad = (head_total * factor).reshape(RECS, C, K, C)
    return (target_grad, head_grad)
```

```python
import math

import jax
import jax.numpy as jnp
from jax import lax
from jax.experimental import pallas as pl
from jax.experimental.pallas import tpu as pltpu
from jax.sharding import Mesh, PartitionSpec as P

BF = jnp.bfloat16
F32 = jnp.float32
Z_ORDER = (4, 3, -3, 2, -2, 1, -1, 0)
Z_BUNDLES = (3, 4, 1)


def gelu_exact(values):
    return jax.nn.gelu(values, approximate=False)


def encode(piece, conv_first, conv_second, conv_third, enc_gain, ctx_weight):
    channels = conv_first.shape[1]
    positions = piece.shape[0] // 20
    frames = piece.reshape(4 * positions, 5)
    hidden_one = gelu_exact(jnp.dot(frames, conv_first, preferred_element_type=F32)).astype(BF)
    hidden_two = gelu_exact(
        jnp.dot(
            hidden_one.reshape(2 * positions, 2 * channels),
            conv_second,
            preferred_element_type=F32,
        )
    ).astype(BF)
    mixed = jnp.dot(
        hidden_two.reshape(positions, 2 * channels), conv_third, preferred_element_type=F32
    )
    average = jnp.mean(mixed, -1, keepdims=True)
    centred = mixed - average
    variance = jnp.mean(centred * centred, -1, keepdims=True)
    latent = (centred / jnp.sqrt(variance + 1e-05) * enc_gain).astype(BF)
    latent_wide = latent.astype(F32)
    target = (
        latent_wide / jnp.sqrt(jnp.sum(latent_wide * latent_wide, -1, keepdims=True) + 1e-06)
    ).astype(BF)
    context = latent
    for layer_index in range(ctx_weight.shape[0]):
        dilation = 2**layer_index
        before = jnp.concatenate(
            [jnp.zeros((dilation, channels), BF), context[: positions - dilation]], 0
        )
        joined = jnp.concatenate([context, before], 1)
        update = gelu_exact(jnp.dot(joined, ctx_weight[layer_index], preferred_element_type=F32))
        context = (context.astype(F32) + update).astype(BF)
    return (target, context)


def score_kernel(
    where_ref, tgt_ref, ctx_ref, hw_ref, *rest, horizon, groups, per_group, positions, bank_count
):
    banks = rest[:bank_count]
    keep_ref, send_ref, hkeep_ref, hsend_ref, pos_ref = rest[bank_count : bank_count + 5]
    nbuf, q_s, t_s, pg_s, p_s, inv_s, sc_s, pad_s, sems = rest[bank_count + 5 :]
    rows = positions // groups
    entries = groups * per_group

    def start(e, carry):
        bank_id = where_ref[0, e]
        row = where_ref[1, e]
        for a in range(bank_count):

            @pl.when(bank_id == a)
            def _():
                pltpu.make_async_copy(banks[a].at[row], nbuf.at[e], sems.at[e]).start()

        return carry

    lax.fori_loop(0, entries, start, 0)

    keep_ref[...] = jnp.zeros(keep_ref.shape, BF)
    send_ref[...] = jnp.zeros(send_ref.shape, BF)

    pad_s[:positions] = tgt_ref[...].astype(F32)
    pad_s[positions:] = jnp.zeros((16, pad_s.shape[1]), F32)
    for k in range(horizon):
        pred = jnp.dot(ctx_ref[...], hw_ref[k], preferred_element_type=F32)
        inv = 1.0 / jnp.sqrt(jnp.sum(pred * pred, -1, keepdims=True) + 1e-06)
        query = (pred * inv).astype(BF)
        shifted = pad_s[k + 1 : k + 1 + positions]
        score = 10.0 * jnp.sum(query.astype(F32) * shifted, -1, keepdims=True)
        part = slice(k * rows, (k + 1) * rows)
        q_s[:, part, :] = query.reshape(groups, rows, -1)
        t_s[:, part, :] = shifted.astype(BF).reshape(groups, rows, -1)
        inv_s[:, part, :] = inv.reshape(groups, rows, 1)
        sc_s[:, part, :] = score.reshape(groups, rows, 1)

    row_id = lax.broadcasted_iota(jnp.int32, (horizon * rows, 1), 0)
    step_id = row_id // rows
    local_id = row_id - step_id * rows

    def group(g, carry):
        for s in range(per_group):
            e = g * per_group + s
            pltpu.make_async_copy(banks[0].at[0], nbuf.at[e], sems.at[e]).wait()
        queries = q_s[g]
        negatives = nbuf[pl.ds(g * per_group, per_group)].reshape(per_group * 128, -1)
        negative = lax.dot_general(
            queries, negatives, (((1,), (1,)), ((), ())), preferred_element_type=F32
        )
        neg_exp = jnp.exp(10.0 * negative)
        pos_exp = jnp.exp(sc_s[g])
        partition = pos_exp + jnp.sum(neg_exp, -1, keepdims=True)
        usable = ((g * rows + local_id + step_id + 1) < positions).astype(F32)
        over = 10.0 * usable / partition
        weight = (neg_exp * over).astype(BF)
        pos_weight = pos_exp * over - 10.0 * usable
        neg_part = jnp.dot(weight, negatives, preferred_element_type=F32)
        neg_grad = lax.dot_general(
            weight, queries, (((0,), (0,)), ((), ())), preferred_element_type=F32
        )
        for s in range(per_group):
            e = g * per_group + s
            place = where_ref[2, e]
            block = neg_grad[s * 128 : (s + 1) * 128]

            @pl.when(where_ref[3, e] == 0)
            def _():
                keep_ref[place] = (keep_ref[place].astype(F32) + block).astype(BF)

            @pl.when(where_ref[3, e] != 0)
            def _():
                send_ref[place] = (send_ref[place].astype(F32) + block).astype(BF)

        unit = queries.astype(F32)
        query_grad = pos_weight * t_s[g].astype(F32) + neg_part
        radial = jnp.sum(unit * query_grad, -1, keepdims=True)
        pred_grad = ((query_grad - unit * radial) * inv_s[g]).astype(BF)
        pos_term = pos_weight * unit
        at = pl.ds(pl.multiple_of(g * rows, rows), rows)
        for k in range(horizon):
            pg_s[k, at, :] = pred_grad[k * rows : (k + 1) * rows]
            p_s[k, at, :] = pos_term[k * rows : (k + 1) * rows]
        return carry

    lax.fori_loop(0, groups, group, 0)

    core = where_ref[4, 0]
    half = horizon // 2

    def head(i, carry):
        for ref, base in ((hkeep_ref, core), (hsend_ref, 1 - core)):
            part = lax.dot_general(
                ctx_ref[...],
                pg_s[base * half + i],
                (((0,), (0,)), ((), ())),
                preferred_element_type=F32,
            )
            ref[i] = part.astype(BF)
        return carry

    lax.fori_loop(0, half, head, 0)
    pad_s[...] = jnp.zeros(pad_s.shape, F32)
    for k in range(horizon):
        at = slice(k + 1, k + 1 + positions)
        pad_s[at] = pad_s[at] + p_s[k]
    pos_ref[...] = pad_s[:positions]


def score(where, target, context, head_maps, banks, groups, per_group):
    positions, channels = target.shape
    horizon = head_maps.shape[0]
    blocks = 2 * (positions // 128) * banks[0].shape[0]
    rows = horizon * positions // groups
    vmem = pl.BlockSpec(memory_space=pltpu.VMEM)
    hbm = pl.BlockSpec(memory_space=pl.ANY)
    return pl.pallas_call(
        lambda *refs: score_kernel(
            *refs,
            horizon=horizon,
            groups=groups,
            per_group=per_group,
            positions=positions,
            bank_count=len(banks),
        ),
        out_shape=(
            jax.ShapeDtypeStruct((blocks, 128, channels), BF),
            jax.ShapeDtypeStruct((blocks, 128, channels), BF),
            jax.ShapeDtypeStruct((horizon // 2, channels, channels), BF),
            jax.ShapeDtypeStruct((horizon // 2, channels, channels), BF),
            jax.ShapeDtypeStruct((positions, channels), F32),
        ),
        in_specs=[pl.BlockSpec(memory_space=pltpu.SMEM), vmem, vmem, vmem] + [hbm] * len(banks),
        out_specs=(vmem,) * 5,
        scratch_shapes=[
            pltpu.VMEM((groups * per_group, 128, channels), BF),
            pltpu.VMEM((groups, rows, channels), BF),
            pltpu.VMEM((groups, rows, channels), BF),
            pltpu.VMEM((horizon, positions, channels), BF),
            pltpu.VMEM((horizon, positions, channels), F32),
            pltpu.VMEM((groups, rows, 1), F32),
            pltpu.VMEM((groups, rows, 1), F32),
            pltpu.VMEM((positions + 16, channels), F32),
            pltpu.SemaphoreType.DMA((groups * per_group,)),
        ],
        name="score",
    )(where, target, context, head_maps, *banks)


def shift(values, axis, by):
    size = lax.axis_size(axis)
    return lax.ppermute(values, axis, [(i, (i + by) % size) for i in range(size)])


def exchange(values, axis):
    return lax.all_to_all(values, axis, 0, 0, tiled=True)


def add(*terms):
    total = terms[0].astype(F32)
    for term in terms[1:]:
        total = total + term.astype(F32)
    return total


def gather_targets(target):
    z_size = lax.axis_size("z")
    row = exchange(jnp.broadcast_to(target[None], (z_size,) + target.shape), "z")
    left = shift(row, "x", 1)
    right = shift(row, "x", -1)
    far_low = shift(left[:, :128], "x", 1)
    far_high = shift(right[:, 128:], "x", -1)
    mine = [row, left, right, far_low, far_high]
    return mine + [shift(v, "c", 1) for v in mine]


def reduce_x(here, ahead, behind, far):
    low = shift(far[:, :128], "x", 1)
    high = shift(far[:, 128:], "x", -1)
    ahead = jnp.concatenate([add(ahead[:, :128], low).astype(BF), ahead[:, 128:]], 1)
    behind = jnp.concatenate([behind[:, :128], add(behind[:, 128:], high).astype(BF)], 1)
    return add(here, shift(ahead, "x", 1), shift(behind, "x", -1))


def return_blocks(keep, send):
    received = shift(send, "c", 1)
    total = None
    first = 0
    for count in Z_BUNDLES:
        parts = [
            add(keep[d, first : first + count], received[d, first : first + count]).astype(BF)
            for d in (0, 1, 3, 2)
        ]
        sums = reduce_x(*parts)
        for i in range(count):
            by = Z_ORDER[first + i]
            term = sums[i] if by == 0 else shift(sums[i].astype(BF), "z", by).astype(F32)
            total = term if total is None else total + term
        first += count
    return total


def reduce_heads(keep, send):
    x_size, z_size = lax.axis_size("x"), lax.axis_size("z")
    channels = keep.shape[-1]
    part = add(keep, shift(send, "c", 1)).astype(BF).reshape(x_size, z_size, -1, channels)
    part = jnp.sum(exchange(part, "x").astype(F32), 0).astype(BF)
    part = jnp.sum(exchange(part, "z").astype(F32), 0).astype(BF)
    part = exchange(jnp.broadcast_to(part[None], (z_size,) + part.shape), "z")
    part = exchange(jnp.broadcast_to(part[None], (x_size,) + part.shape), "x")
    part = part.reshape(keep.shape)
    other = shift(part, "c", 1)
    core = lax.axis_index("c")
    return jnp.concatenate(
        [jnp.where(core == 0, part, other), jnp.where(core == 0, other, part)], 0
    )


def local(ecg, conv_first, conv_second, conv_third, enc_gain, ctx_weight, head_weight, sources):
    z_size, x_size, c_size = (lax.axis_size(a) for a in ("z", "x", "c"))
    groups, per_group = sources.shape[1:3]
    z_id, x_id, c_id = (lax.axis_index(a) for a in ("z", "x", "c"))
    owner = sources[0, :, :, 0].reshape(-1)
    block = sources[0, :, :, 1].reshape(-1)
    owner_z = owner // (x_size * c_size)
    owner_x = (owner // c_size) % x_size
    other_core = (owner % c_size != c_id).astype(jnp.int32)
    dx = (owner_x - x_id) % x_size
    dz = (owner_z - z_id) % z_size
    bank = jnp.where(
        dx == 0, 0, jnp.where(dx == 3, 1, jnp.where(dx == 1, 2, 3 + block))
    ) + 5 * other_core
    bank_row = jnp.where(dx == 2, owner_z, 2 * owner_z + block)
    position = jnp.where(dz == 0, 7, jnp.where(dz == 4, 0, jnp.where(dz < 4, 7 - 2 * dz, 2 * dz - 8)))
    place = 2 * (dx * z_size + position) + block
    where = jnp.stack(
        [bank, bank_row, place, other_core, jnp.full_like(bank, 0) + c_id]
    ).astype(jnp.int32)

    target, context = encode(
        ecg.reshape(-1), conv_first, conv_second, conv_third, enc_gain, ctx_weight
    )
    positions, channels = target.shape
    horizon = head_weight.shape[1]
    banks = [v.reshape(-1, 128, channels) for v in gather_targets(target)]
    keep, send, head_keep, head_send, pos_grad = score(
        where, target, context, head_weight.transpose(1, 0, 2), banks, groups, per_group
    )
    shape = (x_size, z_size, positions, channels)
    summed = return_blocks(keep.reshape(shape), send.reshape(shape))
    target_grad = ((pos_grad + summed) / horizon)[None]
    heads = reduce_heads(head_keep, head_send)
    factor = math.sqrt(channels / (z_size * x_size * c_size * positions))
    head_grad = (heads.astype(F32) * factor).transpose(1, 0, 2)[None]
    return (target_grad, head_grad)


def solution(mesh):
    fine = Mesh(mesh.devices.reshape(8, 4, 2, -1), ("z", "x", "c", "rep"))
    dp = ("z", "x", "c")
    in_specs = (P("rep", dp), P(), P(), P(), P(), P(), P(), P("rep", dp, None, None))
    out_specs = (P("rep", dp, None), P("rep", None, None, None))
    return jax.shard_map(local, mesh=fine, in_specs=in_specs, out_specs=out_specs, check_vma=False)
```

```python
import math

import jax
import jax.numpy as jnp
from jax import lax
from jax.experimental import pallas as pl
from jax.experimental.pallas import tpu as pltpu
from jax.sharding import Mesh, PartitionSpec as P

BF = jnp.bfloat16
F32 = jnp.float32
Z_ORDER = (4, 3, -3, 2, -2, 1, -1, 0)
Z_BUNDLES = (4, 4)


def gelu_exact(values):
    return jax.nn.gelu(values, approximate=False)


def encode(piece, conv_first, conv_second, conv_third, enc_gain, ctx_weight):
    channels = conv_first.shape[1]
    positions = piece.shape[0] // 20
    frames = piece.reshape(4 * positions, 5)
    hidden_one = gelu_exact(jnp.dot(frames, conv_first, preferred_element_type=F32)).astype(BF)
    hidden_two = gelu_exact(
        jnp.dot(
            hidden_one.reshape(2 * positions, 2 * channels),
            conv_second,
            preferred_element_type=F32,
        )
    ).astype(BF)
    mixed = jnp.dot(
        hidden_two.reshape(positions, 2 * channels), conv_third, preferred_element_type=F32
    )
    average = jnp.mean(mixed, -1, keepdims=True)
    centred = mixed - average
    variance = jnp.mean(centred * centred, -1, keepdims=True)
    latent = (centred / jnp.sqrt(variance + 1e-05) * enc_gain).astype(BF)
    latent_wide = latent.astype(F32)
    target = (
        latent_wide / jnp.sqrt(jnp.sum(latent_wide * latent_wide, -1, keepdims=True) + 1e-06)
    ).astype(BF)
    context = latent
    for layer_index in range(ctx_weight.shape[0]):
        dilation = 2**layer_index
        before = jnp.concatenate(
            [jnp.zeros((dilation, channels), BF), context[: positions - dilation]], 0
        )
        joined = jnp.concatenate([context, before], 1)
        update = gelu_exact(jnp.dot(joined, ctx_weight[layer_index], preferred_element_type=F32))
        context = (context.astype(F32) + update).astype(BF)
    return (target, context)


def query_kernel(tgt_ref, ctx_ref, hw_ref, q_ref, t_ref, inv_ref, sc_ref, pad_s, *, groups):
    positions, channels = tgt_ref.shape
    horizon = hw_ref.shape[0]
    rows = positions // groups
    pad_s[:positions] = tgt_ref[...].astype(F32)
    pad_s[positions:] = jnp.zeros((16, channels), F32)
    for k in range(horizon):
        pred = jnp.dot(ctx_ref[...], hw_ref[k], preferred_element_type=F32)
        inv = 1.0 / jnp.sqrt(jnp.sum(pred * pred, -1, keepdims=True) + 1e-06)
        query = (pred * inv).astype(BF)
        shifted = pad_s[k + 1 : k + 1 + positions]
        score = 10.0 * jnp.sum(query.astype(F32) * shifted, -1, keepdims=True)
        part = slice(k * rows, (k + 1) * rows)
        q_ref[:, part, :] = query.reshape(groups, rows, -1)
        t_ref[:, part, :] = shifted.astype(BF).reshape(groups, rows, -1)
        inv_ref[:, part, :] = inv.reshape(groups, rows, 1)
        sc_ref[:, part, :] = score.reshape(groups, rows, 1)


def score_kernel(where_ref, q_ref, t_ref, inv_ref, sc_ref, *rest, positions, per_group, bank_count):
    banks = rest[:bank_count]
    keep_ref, send_ref, pg_ref, p_ref = rest[bank_count : bank_count + 4]
    nbuf, sems = rest[bank_count + 4 :]
    groups, queries_count, _ = q_ref.shape
    horizon = pg_ref.shape[0]
    rows = positions // groups
    entries = groups * per_group

    def start(e, carry):
        bank_id = where_ref[0, e]
        row = where_ref[1, e]
        for a in range(bank_count):

            @pl.when(bank_id == a)
            def _():
                pltpu.make_async_copy(banks[a].at[row], nbuf.at[e], sems.at[e]).start()

        return carry

    lax.fori_loop(0, entries, start, 0)
    keep_ref[...] = jnp.zeros(keep_ref.shape, BF)
    send_ref[...] = jnp.zeros(send_ref.shape, BF)
    row_id = lax.broadcasted_iota(jnp.int32, (queries_count, 1), 0)
    step_id = row_id // rows
    local_id = row_id - step_id * rows

    def group(g, carry):
        for s in range(per_group):
            e = g * per_group + s
            pltpu.make_async_copy(banks[0].at[0], nbuf.at[e], sems.at[e]).wait()
        queries = q_ref[g]
        negatives = nbuf[pl.ds(g * per_group, per_group)].reshape(per_group * 128, -1)
        negative = lax.dot_general(
            queries, negatives, (((1,), (1,)), ((), ())), preferred_element_type=F32
        )
        neg_exp = jnp.exp(10.0 * negative)
        pos_exp = jnp.exp(sc_ref[g])
        partition = pos_exp + jnp.sum(neg_exp, -1, keepdims=True)
        usable = ((g * rows + local_id + step_id + 1) < positions).astype(F32)
        over = 10.0 * usable / partition
        weight = (neg_exp * over).astype(BF)
        pos_weight = pos_exp * over - 10.0 * usable
        neg_part = jnp.dot(weight, negatives, preferred_element_type=F32)
        neg_grad = lax.dot_general(
            weight, queries, (((0,), (0,)), ((), ())), preferred_element_type=F32
        )
        for s in range(per_group):
            e = g * per_group + s
            place = where_ref[2, e]
            sent = where_ref[3, e].astype(F32)
            block = neg_grad[s * 128 : (s + 1) * 128]
            send_ref[place] = (send_ref[place].astype(F32) + block * sent).astype(BF)
            keep_ref[place] = (keep_ref[place].astype(F32) + block * (1.0 - sent)).astype(BF)

        unit = queries.astype(F32)
        query_grad = pos_weight * t_ref[g].astype(F32) + neg_part
        radial = jnp.sum(unit * query_grad, -1, keepdims=True)
        pred_grad = ((query_grad - unit * radial) * inv_ref[g]).astype(BF)
        pos_term = pos_weight * unit
        at = pl.ds(pl.multiple_of(g * rows, rows), rows)
        for k in range(horizon):
            pg_ref[k, at, :] = pred_grad[k * rows : (k + 1) * rows]
            p_ref[k, at, :] = pos_term[k * rows : (k + 1) * rows]
        return carry

    lax.fori_loop(0, groups, group, 0)


def head_kernel(core_ref, ctx_ref, pg_ref, p_ref, hkeep_ref, hsend_ref, pos_ref, pad_s):
    core = core_ref[0]
    half = hkeep_ref.shape[0]

    def head(i, carry):
        for ref, base in ((hkeep_ref, core), (hsend_ref, 1 - core)):
            part = lax.dot_general(
                ctx_ref[...],
                pg_ref[base * half + i],
                (((0,), (0,)), ((), ())),
                preferred_element_type=F32,
            )
            ref[i] = part.astype(BF)
        return carry

    lax.fori_loop(0, half, head, 0)
    positions = pos_ref.shape[0]
    pad_s[...] = jnp.zeros(pad_s.shape, F32)
    for k in range(p_ref.shape[0]):
        at = slice(k + 1, k + 1 + positions)
        pad_s[at] = pad_s[at] + p_ref[k]
    pos_ref[...] = pad_s[:positions]


def make_queries(target, context, head_maps, groups):
    positions, channels = target.shape
    rows = head_maps.shape[0] * positions // groups
    vmem = pl.BlockSpec(memory_space=pltpu.VMEM)
    return pl.pallas_call(
        lambda *refs: query_kernel(*refs, groups=groups),
        out_shape=(
            jax.ShapeDtypeStruct((groups, rows, channels), BF),
            jax.ShapeDtypeStruct((groups, rows, channels), BF),
            jax.ShapeDtypeStruct((groups, rows, 1), F32),
            jax.ShapeDtypeStruct((groups, rows, 1), F32),
        ),
        in_specs=[vmem] * 3,
        out_specs=(vmem,) * 4,
        scratch_shapes=[pltpu.VMEM((positions + 16, channels), F32)],
        name="queries",
    )(target, context, head_maps)


def score(where, made, banks, horizon, positions, per_group):
    groups, _, channels = made[0].shape
    blocks = 2 * (positions // 128) * banks[0].shape[0]
    vmem = pl.BlockSpec(memory_space=pltpu.VMEM)
    hbm = pl.BlockSpec(memory_space=pl.ANY)
    return pl.pallas_call(
        lambda *refs: score_kernel(
            *refs, positions=positions, per_group=per_group, bank_count=len(banks)
        ),
        out_shape=(
            jax.ShapeDtypeStruct((blocks, 128, channels), BF),
            jax.ShapeDtypeStruct((blocks, 128, channels), BF),
            jax.ShapeDtypeStruct((horizon, positions, channels), BF),
            jax.ShapeDtypeStruct((horizon, positions, channels), F32),
        ),
        in_specs=[pl.BlockSpec(memory_space=pltpu.SMEM)] + [vmem] * 4 + [hbm] * len(banks),
        out_specs=(vmem,) * 4,
        scratch_shapes=[
            pltpu.VMEM((groups * per_group, 128, channels), BF),
            pltpu.SemaphoreType.DMA((groups * per_group,)),
        ],
        name="score",
    )(where, *made, *banks)


def head_product(core, context, pred_grad, pos_terms):
    horizon, positions, channels = pred_grad.shape
    vmem = pl.BlockSpec(memory_space=pltpu.VMEM)
    half = jax.ShapeDtypeStruct((horizon // 2, channels, channels), BF)
    return pl.pallas_call(
        head_kernel,
        out_shape=(half, half, jax.ShapeDtypeStruct((positions, channels), F32)),
        in_specs=[pl.BlockSpec(memory_space=pltpu.SMEM), vmem, vmem, vmem],
        out_specs=(vmem, vmem, vmem),
        scratch_shapes=[pltpu.VMEM((positions + 16, channels), F32)],
        name="heads",
    )(core.reshape(1), context, pred_grad, pos_terms)


def shift(values, axis, by):
    size = lax.axis_size(axis)
    return lax.ppermute(values, axis, [(i, (i + by) % size) for i in range(size)])


def exchange(values, axis):
    return lax.all_to_all(values, axis, 0, 0, tiled=True)


def add(*terms):
    total = terms[0].astype(F32)
    for term in terms[1:]:
        total = total + term.astype(F32)
    return total


def gather_targets(target):
    z_size = lax.axis_size("z")
    row = exchange(jnp.broadcast_to(target[None], (z_size,) + target.shape), "z")
    left = shift(row, "x", 1)
    right = shift(row, "x", -1)
    far_low = shift(left[:, :128], "x", 1)
    far_high = shift(right[:, 128:], "x", -1)
    mine = [row, left, right, far_low, far_high]
    return mine + [shift(v, "c", 1) for v in mine]


def pair(values, axis, bit):
    size = lax.axis_size(axis)
    return lax.ppermute(values, axis, [(i, i ^ bit) for i in range(size)])


def pick(values, axis, at):
    return lax.dynamic_index_in_dim(values, at, axis, keepdims=False)


def join(mine, other, bit, axis):
    low = jnp.where(bit == 0, mine, other)
    high = jnp.where(bit == 0, other, mine)
    return jnp.stack([low, high], axis)


def after(values, other):
    zero = other[(0,) * (other.ndim - 1) + (slice(0, 1),)].astype(F32) * 0.0
    return (values.astype(F32) + zero.reshape(())).astype(values.dtype)


def exchange_back(keep, send, head_keep, head_send):
    x_id, core = lax.axis_index("x"), lax.axis_index("c")
    x_size, channels = lax.axis_size("x"), keep.shape[-1]
    received = shift(send, "c", 1)
    head = add(head_keep, shift(head_send, "c", 1)).astype(BF)
    starts = [sum(Z_BUNDLES[:i]) for i in range(len(Z_BUNDLES))]

    firsts, seconds, terms = [], [], []
    for first, count in zip(starts, Z_BUNDLES):
        span = slice(first, first + count)
        far_low = add(keep[2, span, :128], received[2, span, :128]).astype(BF)
        far_high = add(keep[2, span, 128:], received[2, span, 128:]).astype(BF)
        firsts.append([shift(far_low, "x", 1), shift(far_high, "x", -1)])
    for i, (first, count) in enumerate(zip(starts, Z_BUNDLES)):
        span = slice(first, first + count)
        low, high, keep, received = lax.optimization_barrier((*firsts[i], keep, received))
        ahead = add(keep[1, span], received[1, span])
        behind = add(keep[3, span], received[3, span])
        ahead = jnp.concatenate([add(ahead[:, :128], low), ahead[:, 128:]], 1).astype(BF)
        behind = jnp.concatenate([behind[:, :128], add(behind[:, 128:], high)], 1).astype(BF)
        seconds.append([shift(ahead, "x", 1), shift(behind, "x", -1)])
    for i, (first, count) in enumerate(zip(starts, Z_BUNDLES)):
        span = slice(first, first + count)
        sums = add(keep[0, span], received[0, span], *seconds[i])
        arrived = []
        for j in range(count):
            by = Z_ORDER[first + j]
            arrived.append(sums[j] if by == 0 else shift(sums[j].astype(BF), "z", by))
        terms.append(lax.optimization_barrier(tuple(arrived)))
    total = add(*(term for group in terms for term in group))

    head = head.reshape(x_size, -1, channels)
    shares = [pick(head, 0, x_id)]
    for by in (1, -1, 2):
        shares.append(shift(pick(head, 0, (x_id + by) % x_size), "x", by))
    head = after(add(*shares).astype(BF), firsts[-1][1])
    head = add(head, pair(head, "z", 1)).astype(BF)
    head = add(head, pair(head, "z", 2)).astype(BF)
    head = after(head, seconds[0][1])
    head = add(head, pair(head, "z", 4)).astype(BF)
    head = after(head, terms[0][0])
    pieces = jnp.stack([head] + [shift(head, "x", by) for by in (1, 2, -1)])
    head = jnp.concatenate([pick(pieces, 0, (x_id - x) % x_size) for x in range(x_size)], 0)
    head = after(head.reshape(head_keep.shape), terms[-1][0])
    both = join(head, shift(head, "c", 1), core, 0)
    return total, both.reshape((2 * head_keep.shape[0],) + head_keep.shape[1:])


def local(ecg, conv_first, conv_second, conv_third, enc_gain, ctx_weight, head_weight, sources):
    z_size, x_size, c_size = (lax.axis_size(a) for a in ("z", "x", "c"))
    groups, per_group = sources.shape[1:3]
    z_id, x_id, c_id = (lax.axis_index(a) for a in ("z", "x", "c"))
    owner = sources[0, :, :, 0].reshape(-1)
    block = sources[0, :, :, 1].reshape(-1)
    owner_z = owner // (x_size * c_size)
    owner_x = (owner // c_size) % x_size
    other_core = (owner % c_size != c_id).astype(jnp.int32)
    dx = (owner_x - x_id) % x_size
    dz = (owner_z - z_id) % z_size
    bank = jnp.where(
        dx == 0, 0, jnp.where(dx == 3, 1, jnp.where(dx == 1, 2, 3 + block))
    ) + 5 * other_core
    bank_row = jnp.where(dx == 2, owner_z, 2 * owner_z + block)
    position = jnp.where(dz == 0, 7, jnp.where(dz == 4, 0, jnp.where(dz < 4, 7 - 2 * dz, 2 * dz - 8)))
    place = 2 * (dx * z_size + position) + block
    where = jnp.stack([bank, bank_row, place, other_core]).astype(jnp.int32)

    target, context = encode(
        ecg.reshape(-1), conv_first, conv_second, conv_third, enc_gain, ctx_weight
    )
    positions, channels = target.shape
    horizon = head_weight.shape[1]
    made = make_queries(target, context, head_weight.transpose(1, 0, 2), groups)
    banks = [v.reshape(-1, 128, channels) for v in gather_targets(target)]
    keep, send, pred_grad, pos_terms = score(where, made, banks, horizon, positions, per_group)
    head_keep, head_send, pos_grad = head_product(
        c_id.astype(jnp.int32), context, pred_grad, pos_terms
    )
    shape = (x_size, z_size, positions, channels)
    summed, heads = exchange_back(
        keep.reshape(shape), send.reshape(shape), head_keep, head_send
    )
    target_grad = ((pos_grad + summed) / horizon)[None]
    factor = math.sqrt(channels / (z_size * x_size * c_size * positions))
    head_grad = (heads.astype(F32) * factor).transpose(1, 0, 2)[None]
    return (target_grad, head_grad)


def solution(mesh):
    fine = Mesh(mesh.devices.reshape(8, 4, 2, -1), ("z", "x", "c", "rep"))
    dp = ("z", "x", "c")
    in_specs = (P("rep", dp), P(), P(), P(), P(), P(), P(), P("rep", dp, None, None))
    out_specs = (P("rep", dp, None), P("rep", None, None, None))
    return jax.shard_map(local, mesh=fine, in_specs=in_specs, out_specs=out_specs, check_vma=False)
```

```python
import math

import jax
import jax.numpy as jnp
from jax import lax
from jax.experimental import pallas as pl
from jax.experimental.pallas import tpu as pltpu
from jax.sharding import Mesh, PartitionSpec as P

BF = jnp.bfloat16
F32 = jnp.float32
Z_ORDER = (4, 3, -3, 2, -2, 1, -1, 0)
Z_BUNDLES = (8,)


def gelu_exact(values):
    return jax.nn.gelu(values, approximate=False)


def encode(piece, conv_first, conv_second, conv_third, enc_gain, ctx_weight):
    channels = conv_first.shape[1]
    positions = piece.shape[0] // 20
    frames = piece.reshape(4 * positions, 5)
    hidden_one = gelu_exact(jnp.dot(frames, conv_first, preferred_element_type=F32)).astype(BF)
    hidden_two = gelu_exact(
        jnp.dot(
            hidden_one.reshape(2 * positions, 2 * channels),
            conv_second,
            preferred_element_type=F32,
        )
    ).astype(BF)
    mixed = jnp.dot(
        hidden_two.reshape(positions, 2 * channels), conv_third, preferred_element_type=F32
    )
    average = jnp.mean(mixed, -1, keepdims=True)
    centred = mixed - average
    variance = jnp.mean(centred * centred, -1, keepdims=True)
    latent = (centred / jnp.sqrt(variance + 1e-05) * enc_gain).astype(BF)
    latent_wide = latent.astype(F32)
    target = (
        latent_wide / jnp.sqrt(jnp.sum(latent_wide * latent_wide, -1, keepdims=True) + 1e-06)
    ).astype(BF)
    context = latent
    for layer_index in range(ctx_weight.shape[0]):
        dilation = 2**layer_index
        before = jnp.concatenate(
            [jnp.zeros((dilation, channels), BF), context[: positions - dilation]], 0
        )
        joined = jnp.concatenate([context, before], 1)
        update = gelu_exact(jnp.dot(joined, ctx_weight[layer_index], preferred_element_type=F32))
        context = (context.astype(F32) + update).astype(BF)
    return (target, context)


def query_kernel(
    tgt_ref, ctx_ref, hw_ref, q_ref, t_ref, inv_ref, exp_ref, ten_ref, pad_s, *, groups
):
    positions, channels = tgt_ref.shape
    horizon = hw_ref.shape[0]
    rows = positions // groups
    pad_s[:positions] = tgt_ref[...].astype(F32)
    pad_s[positions:] = jnp.zeros((16, channels), F32)
    position = lax.broadcasted_iota(jnp.int32, (positions, 1), 0)

    unroll = math.gcd(horizon, 3)

    def step(k, ahead):
        pred = jnp.dot(ctx_ref[...], hw_ref[k], preferred_element_type=F32)
        inv = 1.0 / jnp.sqrt(jnp.sum(pred * pred, -1, keepdims=True) + 1e-06)
        query = (pred * inv).astype(BF)
        shifted = pad_s[ahead + 1 : ahead + 1 + positions]
        score = 10.0 * jnp.sum(query.astype(F32) * shifted, -1, keepdims=True)
        usable = jnp.where(position + k + 1 < positions, 10.0, 0.0)
        part = pl.ds(pl.multiple_of(k * rows, rows), rows)
        q_ref[:, part, :] = query.reshape(groups, rows, -1)
        t_ref[:, part, :] = shifted.astype(BF).reshape(groups, rows, -1)
        inv_ref[:, part, :] = inv.reshape(groups, rows, 1)
        exp_ref[:, part, :] = jnp.exp(score).reshape(groups, rows, 1)
        ten_ref[:, part, :] = usable.reshape(groups, rows, 1)

    def steps(i, carry):
        for j in range(unroll):
            step(i * unroll + j, j)
        pad_s[:positions] = pad_s[unroll : unroll + positions]
        return carry

    lax.fori_loop(0, horizon // unroll, steps, 0)


def score_kernel(
    where_ref, q_ref, t_ref, inv_ref, exp_ref, ten_ref, *rest, positions, per_group, bank_count
):
    banks = rest[:bank_count]
    keep_ref, send_ref, pg_ref, p_ref = rest[bank_count : bank_count + 4]
    nbuf, blocks_s, sems, out_sems = rest[bank_count + 4 :]
    groups = q_ref.shape[0]
    horizon = pg_ref.shape[0]
    rows = positions // groups
    entries = groups * per_group

    def start(e, carry):
        bank_id = where_ref[0, e]
        row = where_ref[1, e]
        for a in range(bank_count):

            @pl.when(bank_id == a)
            def _():
                pltpu.make_async_copy(banks[a].at[row], nbuf.at[e], sems.at[e]).start()

        return carry

    lax.fori_loop(0, entries, start, 0)
    blocks_s[...] = jnp.zeros(blocks_s.shape, BF)

    def group(g, carry):
        for s in range(per_group):
            e = g * per_group + s
            pltpu.make_async_copy(banks[0].at[0], nbuf.at[e], sems.at[e]).wait()
        queries = q_ref[g]
        negatives = nbuf[pl.ds(g * per_group, per_group)].reshape(per_group * 128, -1)
        negative = lax.dot_general(
            queries, negatives, (((1,), (1,)), ((), ())), preferred_element_type=F32
        )
        neg_exp = jnp.exp2((10.0 * math.log2(math.e)) * negative)
        pos_exp = exp_ref[g]
        over = ten_ref[g] / (pos_exp + jnp.sum(neg_exp, -1, keepdims=True))
        weight = (neg_exp * over).astype(BF)
        pos_weight = pos_exp * over - ten_ref[g]
        neg_part = jnp.dot(weight, negatives, preferred_element_type=F32)
        neg_grad = lax.dot_general(
            weight, queries, (((0,), (0,)), ((), ())), preferred_element_type=F32
        )
        for s in range(per_group):
            e = g * per_group + s
            place = where_ref[2, e]
            block = neg_grad[s * 128 : (s + 1) * 128]
            blocks_s[place] = (blocks_s[place].astype(F32) + block).astype(BF)

        unit = queries.astype(F32)
        query_grad = pos_weight * t_ref[g].astype(F32) + neg_part
        radial = jnp.sum(unit * query_grad, -1, keepdims=True)
        pred_grad = ((query_grad - unit * radial) * inv_ref[g]).astype(BF)
        pos_term = pos_weight * unit
        at = pl.ds(pl.multiple_of(g * rows, rows), rows)
        for k in range(horizon):
            pg_ref[k, at, :] = pred_grad[k * rows : (k + 1) * rows]
            p_ref[k, at, :] = pos_term[k * rows : (k + 1) * rows]
        return carry

    lax.fori_loop(0, groups, group, 0)
    half = blocks_s.shape[0] // 2
    sent = pltpu.make_async_copy(blocks_s.at[pl.ds(half, half)], send_ref, out_sems.at[0])
    kept = pltpu.make_async_copy(blocks_s.at[pl.ds(0, half)], keep_ref, out_sems.at[1])
    sent.start()
    kept.start()
    sent.wait()
    kept.wait()


def head_kernel(core_ref, ctx_ref, pg_ref, p_ref, hkeep_ref, hsend_ref, pos_ref, pad_s):
    core = core_ref[0]
    half = hkeep_ref.shape[0]

    def head(i, carry):
        for ref, base in ((hkeep_ref, core), (hsend_ref, 1 - core)):
            part = lax.dot_general(
                ctx_ref[...],
                pg_ref[base * half + i],
                (((0,), (0,)), ((), ())),
                preferred_element_type=F32,
            )
            ref[i] = part.astype(BF)
        return carry

    lax.fori_loop(0, half, head, 0)
    positions = pos_ref.shape[0]
    pad_s[...] = jnp.zeros(pad_s.shape, F32)
    for k in range(p_ref.shape[0]):
        at = slice(k + 1, k + 1 + positions)
        pad_s[at] = pad_s[at] + p_ref[k]
    pos_ref[...] = pad_s[:positions]


def make_queries(target, context, head_maps, groups):
    positions, channels = target.shape
    rows = head_maps.shape[0] * positions // groups
    vmem = pl.BlockSpec(memory_space=pltpu.VMEM)
    return pl.pallas_call(
        lambda *refs: query_kernel(*refs, groups=groups),
        out_shape=(
            jax.ShapeDtypeStruct((groups, rows, channels), BF),
            jax.ShapeDtypeStruct((groups, rows, channels), BF),
            jax.ShapeDtypeStruct((groups, rows, 1), F32),
            jax.ShapeDtypeStruct((groups, rows, 1), F32),
            jax.ShapeDtypeStruct((groups, rows, 1), F32),
        ),
        in_specs=[vmem] * 3,
        out_specs=(vmem,) * 5,
        scratch_shapes=[pltpu.VMEM((positions + 16, channels), F32)],
        name="queries",
    )(target, context, head_maps)


def score(where, made, banks, horizon, positions, per_group):
    groups, _, channels = made[0].shape
    blocks = 2 * (positions // 128) * banks[0].shape[0]
    vmem = pl.BlockSpec(memory_space=pltpu.VMEM)
    hbm = pl.BlockSpec(memory_space=pl.ANY)
    return pl.pallas_call(
        lambda *refs: score_kernel(
            *refs, positions=positions, per_group=per_group, bank_count=len(banks)
        ),
        out_shape=(
            jax.ShapeDtypeStruct((blocks, 128, channels), BF),
            jax.ShapeDtypeStruct((blocks, 128, channels), BF),
            jax.ShapeDtypeStruct((horizon, positions, channels), BF),
            jax.ShapeDtypeStruct((horizon, positions, channels), F32),
        ),
        in_specs=[pl.BlockSpec(memory_space=pltpu.SMEM)] + [vmem] * 5 + [hbm] * len(banks),
        out_specs=(hbm, hbm, vmem, vmem),
        scratch_shapes=[
            pltpu.VMEM((groups * per_group, 128, channels), BF),
            pltpu.VMEM((2 * blocks, 128, channels), BF),
            pltpu.SemaphoreType.DMA((groups * per_group,)),
            pltpu.SemaphoreType.DMA((2,)),
        ],
        name="score",
    )(where, *made, *banks)


def head_product(core, context, pred_grad, pos_terms):
    horizon, positions, channels = pred_grad.shape
    vmem = pl.BlockSpec(memory_space=pltpu.VMEM)
    half = jax.ShapeDtypeStruct((horizon // 2, channels, channels), BF)
    return pl.pallas_call(
        head_kernel,
        out_shape=(half, half, jax.ShapeDtypeStruct((positions, channels), F32)),
        in_specs=[pl.BlockSpec(memory_space=pltpu.SMEM), vmem, vmem, vmem],
        out_specs=(vmem, vmem, vmem),
        scratch_shapes=[pltpu.VMEM((positions + 16, channels), F32)],
        name="heads",
    )(core.reshape(1), context, pred_grad, pos_terms)


def shift(values, axis, by):
    size = lax.axis_size(axis)
    return lax.ppermute(values, axis, [(i, (i + by) % size) for i in range(size)])


def exchange(values, axis):
    return lax.all_to_all(values, axis, 0, 0, tiled=True)


def add(*terms):
    total = terms[0].astype(F32)
    for term in terms[1:]:
        total = total + term.astype(F32)
    return total


def gather_targets(target, made):
    z_size = lax.axis_size("z")
    row = exchange(jnp.broadcast_to(target[None], (z_size,) + target.shape), "z")
    left = shift(row, "x", 1)
    right = shift(row, "x", -1)
    left, right, *made = lax.optimization_barrier((left, right, *made))
    far_low = shift(left[:, :128], "x", 1)
    far_high = shift(right[:, 128:], "x", -1)
    mine = [row, left, right, far_low, far_high]
    return mine + [shift(v, "c", 1) for v in mine], made


def pair(values, axis, bit):
    size = lax.axis_size(axis)
    return lax.ppermute(values, axis, [(i, i ^ bit) for i in range(size)])


def pick(values, axis, at):
    return lax.dynamic_index_in_dim(values, at, axis, keepdims=False)


def join(mine, other, bit, axis):
    low = jnp.where(bit == 0, mine, other)
    high = jnp.where(bit == 0, other, mine)
    return jnp.stack([low, high], axis)


def after(values, other):
    zero = other[(0,) * (other.ndim - 1) + (slice(0, 1),)].astype(F32) * 0.0
    return (values.astype(F32) + zero.reshape(())).astype(values.dtype)


def exchange_back(keep, send, head_keep, head_send):
    x_id, core = lax.axis_index("x"), lax.axis_index("c")
    x_size, channels = lax.axis_size("x"), keep.shape[-1]
    received = shift(send, "c", 1)
    head = add(head_keep, shift(head_send, "c", 1)).astype(BF)
    starts = [sum(Z_BUNDLES[:i]) for i in range(len(Z_BUNDLES))]

    firsts, seconds, terms = [], [], []
    for first, count in zip(starts, Z_BUNDLES):
        span = slice(first, first + count)
        far_low = add(keep[2, span, :128], received[2, span, :128]).astype(BF)
        far_high = add(keep[2, span, 128:], received[2, span, 128:]).astype(BF)
        firsts.append([shift(far_low, "x", 1), shift(far_high, "x", -1)])
    for i, (first, count) in enumerate(zip(starts, Z_BUNDLES)):
        span = slice(first, first + count)
        low, high, keep, received = lax.optimization_barrier((*firsts[i], keep, received))
        ahead = add(keep[1, span], received[1, span])
        behind = add(keep[3, span], received[3, span])
        ahead = jnp.concatenate([add(ahead[:, :128], low), ahead[:, 128:]], 1).astype(BF)
        behind = jnp.concatenate([behind[:, :128], add(behind[:, 128:], high)], 1).astype(BF)
        seconds.append([shift(ahead, "x", 1), shift(behind, "x", -1)])
    for i, (first, count) in enumerate(zip(starts, Z_BUNDLES)):
        span = slice(first, first + count)
        sums = add(keep[0, span], received[0, span], *seconds[i])
        arrived = []
        for j in range(count):
            by = Z_ORDER[first + j]
            arrived.append(sums[j] if by == 0 else shift(sums[j].astype(BF), "z", by))
        terms.append(lax.optimization_barrier(tuple(arrived)))
    total = add(*(term for group in terms for term in group))

    head = head.reshape(x_size, -1, channels)
    shares = [pick(head, 0, x_id)]
    for by in (1, -1, 2):
        shares.append(shift(pick(head, 0, (x_id + by) % x_size), "x", by))
    head = add(*shares).astype(BF)
    head = add(head, pair(head, "z", 1)).astype(BF)
    head = after(head, firsts[-1][1])
    head = add(head, pair(head, "z", 2)).astype(BF)
    head = add(head, pair(head, "z", 4)).astype(BF)
    head = after(head, seconds[0][1])
    pieces = jnp.stack([head] + [shift(head, "x", by) for by in (1, 2, -1)])
    head = jnp.concatenate([pick(pieces, 0, (x_id - x) % x_size) for x in range(x_size)], 0)
    head = after(head.reshape(head_keep.shape), terms[-1][0])
    both = join(head, shift(head, "c", 1), core, 0)
    return total, both.reshape((2 * head_keep.shape[0],) + head_keep.shape[1:])


def local(ecg, conv_first, conv_second, conv_third, enc_gain, ctx_weight, head_weight, sources):
    z_size, x_size, c_size = (lax.axis_size(a) for a in ("z", "x", "c"))
    groups, per_group = sources.shape[1:3]
    z_id, x_id, c_id = (lax.axis_index(a) for a in ("z", "x", "c"))
    owner = sources[0, :, :, 0].reshape(-1)
    block = sources[0, :, :, 1].reshape(-1)
    owner_z = owner // (x_size * c_size)
    owner_x = (owner // c_size) % x_size
    other_core = (owner % c_size != c_id).astype(jnp.int32)
    dx = (owner_x - x_id) % x_size
    dz = (owner_z - z_id) % z_size
    bank = jnp.where(
        dx == 0, 0, jnp.where(dx == 3, 1, jnp.where(dx == 1, 2, 3 + block))
    ) + 5 * other_core
    bank_row = jnp.where(dx == 2, owner_z, 2 * owner_z + block)
    position = jnp.where(dz == 0, 7, jnp.where(dz == 4, 0, jnp.where(dz < 4, 7 - 2 * dz, 2 * dz - 8)))
    place = 2 * (dx * z_size + position) + block
    place = place + 2 * x_size * z_size * other_core
    where = jnp.stack([bank, bank_row, place]).astype(jnp.int32)

    target, context = encode(
        ecg.reshape(-1), conv_first, conv_second, conv_third, enc_gain, ctx_weight
    )
    positions, channels = target.shape
    horizon = head_weight.shape[1]
    made = make_queries(target, context, head_weight.transpose(1, 0, 2), groups)
    banks, made = gather_targets(target, made)
    banks = [v.reshape(-1, 128, channels) for v in banks]
    keep, send, pred_grad, pos_terms = score(where, made, banks, horizon, positions, per_group)
    head_keep, head_send, pos_grad = head_product(
        c_id.astype(jnp.int32), context, pred_grad, pos_terms
    )
    shape = (x_size, z_size, positions, channels)
    summed, heads = exchange_back(
        keep.reshape(shape), send.reshape(shape), head_keep, head_send
    )
    target_grad = ((pos_grad + summed) / horizon)[None]
    factor = math.sqrt(channels / (z_size * x_size * c_size * positions))
    head_grad = (heads.astype(F32) * factor).transpose(1, 0, 2)[None]
    return (target_grad, head_grad)


def solution(mesh):
    fine = Mesh(mesh.devices.reshape(8, 4, 2, -1), ("z", "x", "c", "rep"))
    dp = ("z", "x", "c")
    in_specs = (P("rep", dp), P(), P(), P(), P(), P(), P(), P("rep", dp, None, None))
    out_specs = (P("rep", dp, None), P("rep", None, None, None))
    return jax.shard_map(local, mesh=fine, in_specs=in_specs, out_specs=out_specs, check_vma=False)
```

```python
import math

import jax
import jax.numpy as jnp
from jax import lax
from jax.experimental import pallas as pl
from jax.experimental.pallas import tpu as pltpu
from jax.sharding import Mesh, PartitionSpec as P

BF = jnp.bfloat16
F32 = jnp.float32
Z_ORDER = (4, 3, -3, 2, -2, 1, -1, 0)
Z_BUNDLES = (8,)


def gelu_exact(values):
    return jax.nn.gelu(values, approximate=False)


def encode(piece, conv_first, conv_second, conv_third, enc_gain, ctx_weight):
    channels = conv_first.shape[1]
    positions = piece.shape[0] // 20
    frames = piece.reshape(4 * positions, 5)
    hidden_one = gelu_exact(jnp.dot(frames, conv_first, preferred_element_type=F32)).astype(BF)
    hidden_two = gelu_exact(
        jnp.dot(
            hidden_one.reshape(2 * positions, 2 * channels),
            conv_second,
            preferred_element_type=F32,
        )
    ).astype(BF)
    mixed = jnp.dot(
        hidden_two.reshape(positions, 2 * channels), conv_third, preferred_element_type=F32
    )
    average = jnp.mean(mixed, -1, keepdims=True)
    centred = mixed - average
    variance = jnp.mean(centred * centred, -1, keepdims=True)
    latent = (centred / jnp.sqrt(variance + 1e-05) * enc_gain).astype(BF)
    latent_wide = latent.astype(F32)
    target = (
        latent_wide / jnp.sqrt(jnp.sum(latent_wide * latent_wide, -1, keepdims=True) + 1e-06)
    ).astype(BF)
    context = latent
    for layer_index in range(ctx_weight.shape[0]):
        dilation = 2**layer_index
        before = jnp.concatenate(
            [jnp.zeros((dilation, channels), BF), context[: positions - dilation]], 0
        )
        joined = jnp.concatenate([context, before], 1)
        update = gelu_exact(jnp.dot(joined, ctx_weight[layer_index], preferred_element_type=F32))
        context = (context.astype(F32) + update).astype(BF)
    return (target, context)


def query_kernel(tgt_ref, ctx_ref, hw_ref, q_ref, t_ref, stat_ref, pad_s, *, groups):
    positions, channels = tgt_ref.shape
    horizon = hw_ref.shape[0]
    rows = positions // groups
    pad_s[:positions] = tgt_ref[...].astype(F32)
    pad_s[positions:] = jnp.zeros((16, channels), F32)
    position = lax.broadcasted_iota(jnp.int32, (positions, 1), 0)

    unroll = math.gcd(horizon, 3)

    def step(k, ahead):
        pred = jnp.dot(ctx_ref[...], hw_ref[k], preferred_element_type=F32)
        inv = 1.0 / jnp.sqrt(jnp.sum(pred * pred, -1, keepdims=True) + 1e-06)
        query = (pred * inv).astype(BF)
        shifted = pad_s[ahead + 1 : ahead + 1 + positions]
        score = 10.0 * jnp.sum(query.astype(F32) * shifted, -1, keepdims=True)
        usable = jnp.where(position + k + 1 < positions, 10.0, 0.0)
        part = pl.ds(pl.multiple_of(k * rows, rows), rows)
        q_ref[:, part, :] = query.reshape(groups, rows, -1)
        t_ref[:, part, :] = shifted.astype(BF).reshape(groups, rows, -1)
        stat_ref[:, part, 0:1] = inv.reshape(groups, rows, 1)
        stat_ref[:, part, 1:2] = jnp.exp(score).reshape(groups, rows, 1)
        stat_ref[:, part, 2:3] = usable.reshape(groups, rows, 1)

    def steps(i, carry):
        for j in range(unroll):
            step(i * unroll + j, j)
        pad_s[:positions] = pad_s[unroll : unroll + positions]
        return carry

    lax.fori_loop(0, horizon // unroll, steps, 0)


def score_kernel(where_ref, q_ref, t_ref, stat_ref, *rest, per_group, bank_count):
    banks = rest[:bank_count]
    keep_ref, send_ref, pg_ref, p_ref = rest[bank_count : bank_count + 4]
    nbuf, blocks_s, sems, out_sems = rest[bank_count + 4 :]
    batch = q_ref.shape[0]
    horizon = pg_ref.shape[0]
    rows = pg_ref.shape[1] // batch
    entries = nbuf.shape[0]
    at = pl.program_id(0)

    def start(e, carry):
        bank_id = where_ref[0, e]
        row = where_ref[1, e]
        for a in range(bank_count):

            @pl.when(bank_id == a)
            def _():
                pltpu.make_async_copy(banks[a].at[row], nbuf.at[e], sems.at[e]).start()

        return carry

    def arrive(e, carry):
        pltpu.make_async_copy(banks[0].at[0], nbuf.at[e], sems.at[e]).wait()
        return carry

    @pl.when(at == 0)
    def _():
        lax.fori_loop(0, entries, start, 0)
        blocks_s[...] = jnp.zeros(blocks_s.shape, BF)
        lax.fori_loop(0, entries, arrive, 0)

    def weights(j):
        first = (at * batch + j) * per_group
        queries = q_ref[j]
        stat = stat_ref[j]
        pos_exp, ten = stat[:, 1:2], stat[:, 2:3]
        negatives = nbuf[pl.ds(first, per_group)].reshape(per_group * 128, -1)
        negative = lax.dot_general(
            queries, negatives, (((1,), (1,)), ((), ())), preferred_element_type=F32
        )
        neg_exp = jnp.exp2((10.0 * math.log2(math.e)) * negative)
        over = ten / (pos_exp + jnp.sum(neg_exp, -1, keepdims=True))
        weight = (neg_exp * over).astype(BF)
        pos_weight = pos_exp * over - ten
        neg_part = jnp.dot(weight, negatives, preferred_element_type=F32)
        neg_grad = lax.dot_general(
            weight, queries, (((0,), (0,)), ((), ())), preferred_element_type=F32
        )
        return queries, pos_weight, neg_part, neg_grad

    def finish(j, queries, pos_weight, neg_part, neg_grad):
        unit = queries.astype(F32)
        query_grad = pos_weight * t_ref[j].astype(F32) + neg_part
        radial = jnp.sum(unit * query_grad, -1, keepdims=True)
        pred_grad = ((query_grad - unit * radial) * stat_ref[j][:, 0:1]).astype(BF)
        pos_term = (pos_weight * unit).astype(BF)
        for k in range(horizon):
            pg_ref[k, j * rows : (j + 1) * rows, :] = pred_grad[k * rows : (k + 1) * rows]
            p_ref[k, j * rows : (j + 1) * rows, :] = pos_term[k * rows : (k + 1) * rows]
        for s in range(per_group):
            place = where_ref[2, (at * batch + j) * per_group + s]
            block = neg_grad[s * 128 : (s + 1) * 128]
            blocks_s[place] = (blocks_s[place].astype(F32) + block).astype(BF)

    made = [weights(j) for j in range(batch)]
    for j in range(batch):
        finish(j, *made[j])

    @pl.when(at == pl.num_programs(0) - 1)
    def _():
        half = blocks_s.shape[0] // 2
        sent = pltpu.make_async_copy(blocks_s.at[pl.ds(half, half)], send_ref, out_sems.at[0])
        kept = pltpu.make_async_copy(blocks_s.at[pl.ds(0, half)], keep_ref, out_sems.at[1])
        sent.start()
        kept.start()
        sent.wait()
        kept.wait()


def head_kernel(core_ref, ctx_ref, pg_ref, p_ref, hkeep_ref, hsend_ref, pos_ref, pad_s):
    core = core_ref[0]
    half = hkeep_ref.shape[0]

    def head(i, carry):
        for ref, base in ((hkeep_ref, core), (hsend_ref, 1 - core)):
            part = lax.dot_general(
                ctx_ref[...],
                pg_ref[base * half + i],
                (((0,), (0,)), ((), ())),
                preferred_element_type=F32,
            )
            ref[i] = part.astype(BF)
        return carry

    lax.fori_loop(0, half, head, 0)
    positions = pos_ref.shape[0]
    pad_s[...] = jnp.zeros(pad_s.shape, F32)
    for k in range(p_ref.shape[0]):
        at = slice(k + 1, k + 1 + positions)
        pad_s[at] = pad_s[at] + p_ref[k].astype(F32)
    pos_ref[...] = pad_s[:positions]


def make_queries(target, context, head_maps, groups):
    positions, channels = target.shape
    rows = head_maps.shape[0] * positions // groups
    vmem = pl.BlockSpec(memory_space=pltpu.VMEM)
    return pl.pallas_call(
        lambda *refs: query_kernel(*refs, groups=groups),
        out_shape=(
            jax.ShapeDtypeStruct((groups, rows, channels), BF),
            jax.ShapeDtypeStruct((groups, rows, channels), BF),
            jax.ShapeDtypeStruct((groups, rows, 3), F32),
        ),
        in_specs=[vmem] * 3,
        out_specs=(vmem,) * 3,
        scratch_shapes=[pltpu.VMEM((positions + 16, channels), F32)],
        name="queries",
    )(target, context, head_maps)


def score(where, made, banks, horizon, positions, per_group):
    groups, queries, channels = made[0].shape
    blocks = 2 * (positions // 128) * banks[0].shape[0]
    batch = math.gcd(groups, 2)
    span = batch * (positions // groups)
    hbm = pl.BlockSpec(memory_space=pl.ANY)

    def by_group(width):
        return pl.BlockSpec((batch, queries, width), lambda i: (i, 0, 0))

    by_position = pl.BlockSpec((horizon, span, channels), lambda i: (0, i, 0))
    return pl.pallas_call(
        lambda *refs: score_kernel(*refs, per_group=per_group, bank_count=len(banks)),
        grid=(groups // batch,),
        out_shape=(
            jax.ShapeDtypeStruct((blocks, 128, channels), BF),
            jax.ShapeDtypeStruct((blocks, 128, channels), BF),
            jax.ShapeDtypeStruct((horizon, positions, channels), BF),
            jax.ShapeDtypeStruct((horizon, positions, channels), BF),
        ),
        in_specs=[
            pl.BlockSpec(memory_space=pltpu.SMEM),
            by_group(channels),
            by_group(channels),
            by_group(made[2].shape[-1]),
        ]
        + [hbm] * len(banks),
        out_specs=(hbm, hbm, by_position, by_position),
        scratch_shapes=[
            pltpu.VMEM((groups * per_group, 128, channels), BF),
            pltpu.VMEM((2 * blocks, 128, channels), BF),
            pltpu.SemaphoreType.DMA((groups * per_group,)),
            pltpu.SemaphoreType.DMA((2,)),
        ],
        name="score",
    )(where, *made, *banks)


def head_product(core, context, pred_grad, pos_terms):
    horizon, positions, channels = pred_grad.shape
    vmem = pl.BlockSpec(memory_space=pltpu.VMEM)
    half = jax.ShapeDtypeStruct((horizon // 2, channels, channels), BF)
    return pl.pallas_call(
        head_kernel,
        out_shape=(half, half, jax.ShapeDtypeStruct((positions, channels), F32)),
        in_specs=[pl.BlockSpec(memory_space=pltpu.SMEM), vmem, vmem, vmem],
        out_specs=(vmem, vmem, vmem),
        scratch_shapes=[pltpu.VMEM((positions + 16, channels), F32)],
        name="heads",
    )(core.reshape(1), context, pred_grad, pos_terms)


def shift(values, axis, by):
    size = lax.axis_size(axis)
    return lax.ppermute(values, axis, [(i, (i + by) % size) for i in range(size)])


def exchange(values, axis):
    return lax.all_to_all(values, axis, 0, 0, tiled=True)


def add(*terms):
    total = terms[0].astype(F32)
    for term in terms[1:]:
        total = total + term.astype(F32)
    return total


def gather_targets(target, made):
    z_size = lax.axis_size("z")
    row = exchange(jnp.broadcast_to(target[None], (z_size,) + target.shape), "z")
    left = shift(row, "x", 1)
    right = shift(row, "x", -1)
    left, right, *made = lax.optimization_barrier((left, right, *made))
    far_low = shift(left[:, :128], "x", 1)
    far_high = shift(right[:, 128:], "x", -1)
    mine = [row, left, right, far_low, far_high]
    return mine + [shift(v, "c", 1) for v in mine], made


def pair(values, axis, bit):
    size = lax.axis_size(axis)
    return lax.ppermute(values, axis, [(i, i ^ bit) for i in range(size)])


def pick(values, axis, at):
    return lax.dynamic_index_in_dim(values, at, axis, keepdims=False)


def join(mine, other, bit, axis):
    low = jnp.where(bit == 0, mine, other)
    high = jnp.where(bit == 0, other, mine)
    return jnp.stack([low, high], axis)


def after(values, other):
    zero = other[(0,) * (other.ndim - 1) + (slice(0, 1),)].astype(F32) * 0.0
    return (values.astype(F32) + zero.reshape(())).astype(values.dtype)


def exchange_back(keep, send, head_keep, head_send):
    x_id, core = lax.axis_index("x"), lax.axis_index("c")
    x_size, channels = lax.axis_size("x"), keep.shape[-1]
    received = shift(send, "c", 1)
    head = add(head_keep, shift(head_send, "c", 1)).astype(BF)
    starts = [sum(Z_BUNDLES[:i]) for i in range(len(Z_BUNDLES))]

    firsts, seconds, terms = [], [], []
    for first, count in zip(starts, Z_BUNDLES):
        span = slice(first, first + count)
        far_low = add(keep[2, span, :128], received[2, span, :128]).astype(BF)
        far_high = add(keep[2, span, 128:], received[2, span, 128:]).astype(BF)
        firsts.append([shift(far_low, "x", 1), shift(far_high, "x", -1)])
    for i, (first, count) in enumerate(zip(starts, Z_BUNDLES)):
        span = slice(first, first + count)
        low, high, keep, received = lax.optimization_barrier((*firsts[i], keep, received))
        rest = keep.shape[2] - 128
        low = jnp.pad(low, ((0, 0), (0, rest), (0, 0)))
        high = jnp.pad(high, ((0, 0), (rest, 0), (0, 0)))
        ahead = add(keep[1, span], received[1, span], low).astype(BF)
        behind = add(keep[3, span], received[3, span], high).astype(BF)
        seconds.append([shift(ahead, "x", 1), shift(behind, "x", -1)])
    for i, (first, count) in enumerate(zip(starts, Z_BUNDLES)):
        span = slice(first, first + count)
        sums = add(keep[0, span], received[0, span], *seconds[i])
        arrived = []
        for j in range(count):
            by = Z_ORDER[first + j]
            arrived.append(sums[j] if by == 0 else shift(sums[j].astype(BF), "z", by))
        terms.append(lax.optimization_barrier(tuple(arrived)))
    total = add(*(term for group in terms for term in group))

    head = head.reshape(x_size, -1, channels)
    shares = [pick(head, 0, x_id)]
    for by in (1, -1, 2):
        shares.append(shift(pick(head, 0, (x_id + by) % x_size), "x", by))
    head = add(*shares).astype(BF)
    head = add(head, pair(head, "z", 1)).astype(BF)
    head = after(head, firsts[-1][1])
    head = add(head, pair(head, "z", 2)).astype(BF)
    head = add(head, pair(head, "z", 4)).astype(BF)
    head = after(head, seconds[0][1])
    pieces = jnp.stack([head] + [shift(head, "x", by) for by in (1, 2, -1)])
    head = jnp.concatenate([pick(pieces, 0, (x_id - x) % x_size) for x in range(x_size)], 0)
    head = after(head.reshape(head_keep.shape), terms[-1][0])
    both = join(head, shift(head, "c", 1), core, 0)
    return total, both.reshape((2 * head_keep.shape[0],) + head_keep.shape[1:])


def local(ecg, conv_first, conv_second, conv_third, enc_gain, ctx_weight, head_weight, sources):
    z_size, x_size, c_size = (lax.axis_size(a) for a in ("z", "x", "c"))
    groups, per_group = sources.shape[1:3]
    z_id, x_id, c_id = (lax.axis_index(a) for a in ("z", "x", "c"))
    owner = sources[0, :, :, 0].reshape(-1)
    block = sources[0, :, :, 1].reshape(-1)
    owner_z = owner // (x_size * c_size)
    owner_x = (owner // c_size) % x_size
    other_core = (owner % c_size != c_id).astype(jnp.int32)
    dx = (owner_x - x_id) % x_size
    dz = (owner_z - z_id) % z_size
    bank = jnp.where(
        dx == 0, 0, jnp.where(dx == 3, 1, jnp.where(dx == 1, 2, 3 + block))
    ) + 5 * other_core
    bank_row = jnp.where(dx == 2, owner_z, 2 * owner_z + block)
    position = jnp.where(dz == 0, 7, jnp.where(dz == 4, 0, jnp.where(dz < 4, 7 - 2 * dz, 2 * dz - 8)))
    place = 2 * (dx * z_size + position) + block
    place = place + 2 * x_size * z_size * other_core
    where = jnp.stack([bank, bank_row, place]).astype(jnp.int32)

    target, context = encode(
        ecg.reshape(-1), conv_first, conv_second, conv_third, enc_gain, ctx_weight
    )
    positions, channels = target.shape
    horizon = head_weight.shape[1]
    made = make_queries(target, context, head_weight.transpose(1, 0, 2), groups)
    banks, made = gather_targets(target, made)
    banks = [v.reshape(-1, 128, channels) for v in banks]
    keep, send, pred_grad, pos_terms = score(where, made, banks, horizon, positions, per_group)
    head_keep, head_send, pos_grad = head_product(
        c_id.astype(jnp.int32), context, pred_grad, pos_terms
    )
    shape = (x_size, z_size, positions, channels)
    summed, heads = exchange_back(
        keep.reshape(shape), send.reshape(shape), head_keep, head_send
    )
    target_grad = ((pos_grad + summed) / horizon)[None]
    factor = math.sqrt(channels / (z_size * x_size * c_size * positions))
    head_grad = (heads.astype(F32) * factor).transpose(1, 0, 2)[None]
    return (target_grad, head_grad)


def solution(mesh):
    fine = Mesh(mesh.devices.reshape(8, 4, 2, -1), ("z", "x", "c", "rep"))
    dp = ("z", "x", "c")
    in_specs = (P("rep", dp), P(), P(), P(), P(), P(), P(), P("rep", dp, None, None))
    out_specs = (P("rep", dp, None), P("rep", None, None, None))
    return jax.shard_map(local, mesh=fine, in_specs=in_specs, out_specs=out_specs, check_vma=False)
```

```python
import math

import jax
import jax.numpy as jnp
from jax import lax
from jax.experimental import pallas as pl
from jax.experimental.pallas import tpu as pltpu
from jax.sharding import Mesh, PartitionSpec as P

BF = jnp.bfloat16
F32 = jnp.float32
Z_ORDER = (4, 3, -3, 2, -2, 1, -1, 0)
Z_BUNDLES = (8,)


def gelu_exact(values):
    return jax.nn.gelu(values, approximate=False)


def encode(piece, conv_first, conv_second, conv_third, enc_gain, ctx_weight):
    channels = conv_first.shape[1]
    positions = piece.shape[0] // 20
    frames = piece.reshape(4 * positions, 5)
    hidden_one = gelu_exact(jnp.dot(frames, conv_first, preferred_element_type=F32)).astype(BF)
    hidden_two = gelu_exact(
        jnp.dot(
            hidden_one.reshape(2 * positions, 2 * channels),
            conv_second,
            preferred_element_type=F32,
        )
    ).astype(BF)
    mixed = jnp.dot(
        hidden_two.reshape(positions, 2 * channels), conv_third, preferred_element_type=F32
    )
    average = jnp.mean(mixed, -1, keepdims=True)
    centred = mixed - average
    variance = jnp.mean(centred * centred, -1, keepdims=True)
    latent = (centred / jnp.sqrt(variance + 1e-05) * enc_gain).astype(BF)
    latent_wide = latent.astype(F32)
    target = (
        latent_wide / jnp.sqrt(jnp.sum(latent_wide * latent_wide, -1, keepdims=True) + 1e-06)
    ).astype(BF)
    context = latent
    for layer_index in range(ctx_weight.shape[0]):
        dilation = 2**layer_index
        before = jnp.concatenate(
            [jnp.zeros((dilation, channels), BF), context[: positions - dilation]], 0
        )
        joined = jnp.concatenate([context, before], 1)
        update = gelu_exact(jnp.dot(joined, ctx_weight[layer_index], preferred_element_type=F32))
        context = (context.astype(F32) + update).astype(BF)
    return (target, context)


def query_kernel(tgt_ref, ctx_ref, hw_ref, q_ref, t_ref, stat_ref, pad_s, *, groups):
    positions, channels = tgt_ref.shape
    horizon = hw_ref.shape[0]
    rows = positions // groups
    pad_s[:positions] = tgt_ref[...].astype(F32)
    pad_s[positions:] = jnp.zeros((16, channels), F32)
    position = lax.broadcasted_iota(jnp.int32, (positions, 1), 0)

    unroll = math.gcd(horizon, 3)

    def step(k, ahead):
        pred = jnp.dot(ctx_ref[...], hw_ref[k], preferred_element_type=F32)
        inv = 1.0 / jnp.sqrt(jnp.sum(pred * pred, -1, keepdims=True) + 1e-06)
        query = (pred * inv).astype(BF)
        shifted = pad_s[ahead + 1 : ahead + 1 + positions]
        score = 10.0 * jnp.sum(query.astype(F32) * shifted, -1, keepdims=True)
        usable = jnp.where(position + k + 1 < positions, 10.0, 0.0)
        part = pl.ds(pl.multiple_of(k * rows, rows), rows)
        q_ref[:, part, :] = query.reshape(groups, rows, -1)
        t_ref[:, part, :] = shifted.astype(BF).reshape(groups, rows, -1)
        stat_ref[:, part, 0:1] = inv.reshape(groups, rows, 1)
        stat_ref[:, part, 1:2] = jnp.exp(score).reshape(groups, rows, 1)
        stat_ref[:, part, 2:3] = usable.reshape(groups, rows, 1)

    def steps(i, carry):
        for j in range(unroll):
            step(i * unroll + j, j)
        pad_s[:positions] = pad_s[unroll : unroll + positions]
        return carry

    lax.fori_loop(0, horizon // unroll, steps, 0)


def score_kernel(where_ref, q_ref, t_ref, stat_ref, *rest, per_group, bank_count):
    banks = rest[:bank_count]
    keep_ref, send_ref, pg_ref, p_ref = rest[bank_count : bank_count + 4]
    nbuf, blocks_s, sems, out_sems = rest[bank_count + 4 :]
    batch = q_ref.shape[0]
    horizon = pg_ref.shape[0]
    rows = pg_ref.shape[1] // batch
    entries = nbuf.shape[0]
    at = pl.program_id(0)

    def start(e, carry):
        bank_id = where_ref[0, e]
        row = where_ref[1, e]
        for a in range(bank_count):

            @pl.when(bank_id == a)
            def _():
                pltpu.make_async_copy(banks[a].at[row], nbuf.at[e], sems.at[e]).start()

        return carry

    def arrive(e, carry):
        pltpu.make_async_copy(banks[0].at[0], nbuf.at[e], sems.at[e]).wait()
        return carry

    @pl.when(at == 0)
    def _():
        lax.fori_loop(0, entries, start, 0)
        blocks_s[...] = jnp.zeros(blocks_s.shape, BF)
        lax.fori_loop(0, entries, arrive, 0)

    def weights(j):
        first = (at * batch + j) * per_group
        queries = q_ref[j]
        stat = stat_ref[j]
        pos_exp, ten = stat[:, 1:2], stat[:, 2:3]
        negatives = nbuf[pl.ds(first, per_group)].reshape(per_group * 128, -1)
        negative = lax.dot_general(
            queries, negatives, (((1,), (1,)), ((), ())), preferred_element_type=F32
        )
        neg_exp = jnp.exp2((10.0 * math.log2(math.e)) * negative)
        over = ten / (pos_exp + jnp.sum(neg_exp, -1, keepdims=True))
        weight = (neg_exp * over).astype(BF)
        pos_weight = pos_exp * over - ten
        neg_part = jnp.dot(weight, negatives, preferred_element_type=F32)
        neg_grad = lax.dot_general(
            weight, queries, (((0,), (0,)), ((), ())), preferred_element_type=F32
        )
        return queries, pos_weight, neg_part, neg_grad

    def finish(j, queries, pos_weight, neg_part, neg_grad):
        unit = queries.astype(F32)
        query_grad = pos_weight * t_ref[j].astype(F32) + neg_part
        radial = jnp.sum(unit * query_grad, -1, keepdims=True)
        pred_grad = ((query_grad - unit * radial) * stat_ref[j][:, 0:1]).astype(BF)
        pos_term = (pos_weight * unit).astype(BF)
        for k in range(horizon):
            pg_ref[k, j * rows : (j + 1) * rows, :] = pred_grad[k * rows : (k + 1) * rows]
            p_ref[k, j * rows : (j + 1) * rows, :] = pos_term[k * rows : (k + 1) * rows]
        for s in range(per_group):
            place = where_ref[2, (at * batch + j) * per_group + s]
            block = neg_grad[s * 128 : (s + 1) * 128]
            blocks_s[place] = (blocks_s[place].astype(F32) + block).astype(BF)

    made = [weights(j) for j in range(batch)]
    for j in range(batch):
        finish(j, *made[j])

    @pl.when(at == pl.num_programs(0) - 1)
    def _():
        half = blocks_s.shape[0] // 2
        sent = pltpu.make_async_copy(blocks_s.at[pl.ds(half, half)], send_ref, out_sems.at[0])
        kept = pltpu.make_async_copy(blocks_s.at[pl.ds(0, half)], keep_ref, out_sems.at[1])
        sent.start()
        kept.start()
        sent.wait()
        kept.wait()


def head_kernel(core_ref, ctx_ref, pg_ref, p_ref, hkeep_ref, hsend_ref, pos_ref, pad_s):
    core = core_ref[0]
    half = hkeep_ref.shape[0]

    def head(i, carry):
        for ref, base in ((hkeep_ref, core), (hsend_ref, 1 - core)):
            part = lax.dot_general(
                ctx_ref[...],
                pg_ref[base * half + i],
                (((0,), (0,)), ((), ())),
                preferred_element_type=F32,
            )
            ref[i] = part.astype(BF)
        return carry

    lax.fori_loop(0, half, head, 0)
    positions = pos_ref.shape[0]
    pad_s[...] = jnp.zeros(pad_s.shape, F32)
    for k in range(p_ref.shape[0]):
        at = slice(k + 1, k + 1 + positions)
        pad_s[at] = pad_s[at] + p_ref[k].astype(F32)
    pos_ref[...] = pad_s[:positions]


def make_queries(target, context, head_maps, groups):
    positions, channels = target.shape
    rows = head_maps.shape[0] * positions // groups
    vmem = pl.BlockSpec(memory_space=pltpu.VMEM)
    return pl.pallas_call(
        lambda *refs: query_kernel(*refs, groups=groups),
        out_shape=(
            jax.ShapeDtypeStruct((groups, rows, channels), BF),
            jax.ShapeDtypeStruct((groups, rows, channels), BF),
            jax.ShapeDtypeStruct((groups, rows, 3), F32),
        ),
        in_specs=[vmem] * 3,
        out_specs=(vmem,) * 3,
        scratch_shapes=[pltpu.VMEM((positions + 16, channels), F32)],
        name="queries",
    )(target, context, head_maps)


def score(where, made, banks, horizon, positions, per_group):
    groups, queries, channels = made[0].shape
    blocks = 2 * (positions // 128) * banks[0].shape[0]
    batch = math.gcd(groups, 2)
    span = batch * (positions // groups)
    hbm = pl.BlockSpec(memory_space=pl.ANY)

    def by_group(width):
        return pl.BlockSpec((batch, queries, width), lambda i: (i, 0, 0))

    by_position = pl.BlockSpec((horizon, span, channels), lambda i: (0, i, 0))
    return pl.pallas_call(
        lambda *refs: score_kernel(*refs, per_group=per_group, bank_count=len(banks)),
        grid=(groups // batch,),
        out_shape=(
            jax.ShapeDtypeStruct((blocks, 128, channels), BF),
            jax.ShapeDtypeStruct((blocks, 128, channels), BF),
            jax.ShapeDtypeStruct((horizon, positions, channels), BF),
            jax.ShapeDtypeStruct((horizon, positions, channels), BF),
        ),
        in_specs=[
            pl.BlockSpec(memory_space=pltpu.SMEM),
            by_group(channels),
            by_group(channels),
            by_group(made[2].shape[-1]),
        ]
        + [hbm] * len(banks),
        out_specs=(hbm, hbm, by_position, by_position),
        scratch_shapes=[
            pltpu.VMEM((groups * per_group, 128, channels), BF),
            pltpu.VMEM((2 * blocks, 128, channels), BF),
            pltpu.SemaphoreType.DMA((groups * per_group,)),
            pltpu.SemaphoreType.DMA((2,)),
        ],
        name="score",
    )(where, *made, *banks)


def head_product(core, context, pred_grad, pos_terms):
    horizon, positions, channels = pred_grad.shape
    vmem = pl.BlockSpec(memory_space=pltpu.VMEM)
    half = jax.ShapeDtypeStruct((horizon // 2, channels, channels), BF)
    return pl.pallas_call(
        head_kernel,
        out_shape=(half, half, jax.ShapeDtypeStruct((positions, channels), F32)),
        in_specs=[pl.BlockSpec(memory_space=pltpu.SMEM), vmem, vmem, vmem],
        out_specs=(vmem, vmem, vmem),
        scratch_shapes=[pltpu.VMEM((positions + 16, channels), F32)],
        name="heads",
    )(core.reshape(1), context, pred_grad, pos_terms)


def shift(values, axis, by):
    size = lax.axis_size(axis)
    return lax.ppermute(values, axis, [(i, (i + by) % size) for i in range(size)])


def exchange(values, axis):
    return lax.all_to_all(values, axis, 0, 0, tiled=True)


def add(*terms):
    total = terms[0].astype(F32)
    for term in terms[1:]:
        total = total + term.astype(F32)
    return total


def gather_targets(target, made):
    z_size = lax.axis_size("z")
    row = exchange(jnp.broadcast_to(target[None], (z_size,) + target.shape), "z")
    left = shift(row, "x", 1)
    right = shift(row, "x", -1)
    left, right, *made = lax.optimization_barrier((left, right, *made))
    far_low = shift(left[: z_size // 2], "x", 1)
    far_high = shift(right[z_size // 2 :], "x", -1)
    mine = [row, left, right, far_low, far_high]
    return mine + [shift(v, "c", 1) for v in mine], made


def pair(values, axis, bit):
    size = lax.axis_size(axis)
    return lax.ppermute(values, axis, [(i, i ^ bit) for i in range(size)])


def pick(values, axis, at):
    return lax.dynamic_index_in_dim(values, at, axis, keepdims=False)


def join(mine, other, bit, axis):
    low = jnp.where(bit == 0, mine, other)
    high = jnp.where(bit == 0, other, mine)
    return jnp.stack([low, high], axis)


def after(values, other):
    zero = other[(0,) * (other.ndim - 1) + (slice(0, 1),)].astype(F32) * 0.0
    return (values.astype(F32) + zero.reshape(())).astype(values.dtype)


def exchange_back(keep, send, head_keep, head_send):
    x_id, core = lax.axis_index("x"), lax.axis_index("c")
    x_size, channels = lax.axis_size("x"), keep.shape[-1]
    received = shift(send, "c", 1)
    head = add(head_keep, shift(head_send, "c", 1)).astype(BF)
    starts = [sum(Z_BUNDLES[:i]) for i in range(len(Z_BUNDLES))]

    firsts, seconds, terms = [], [], []
    for first, count in zip(starts, Z_BUNDLES):
        span = slice(first, first + count)
        far_low = add(keep[2, span, :128], received[2, span, :128]).astype(BF)
        far_high = add(keep[2, span, 128:], received[2, span, 128:]).astype(BF)
        firsts.append([shift(far_low, "x", 1), shift(far_high, "x", -1)])
    for i, (first, count) in enumerate(zip(starts, Z_BUNDLES)):
        span = slice(first, first + count)
        low, high, keep, received = lax.optimization_barrier((*firsts[i], keep, received))
        rest = keep.shape[2] - 128
        low = jnp.pad(low, ((0, 0), (0, rest), (0, 0)))
        high = jnp.pad(high, ((0, 0), (rest, 0), (0, 0)))
        ahead = add(keep[1, span], received[1, span], low).astype(BF)
        behind = add(keep[3, span], received[3, span], high).astype(BF)
        seconds.append([shift(ahead, "x", 1), shift(behind, "x", -1)])
    for i, (first, count) in enumerate(zip(starts, Z_BUNDLES)):
        span = slice(first, first + count)
        sums = add(keep[0, span], received[0, span], *seconds[i])
        arrived = []
        for j in range(count):
            by = Z_ORDER[first + j]
            arrived.append(sums[j] if by == 0 else shift(sums[j].astype(BF), "z", by))
        terms.append(lax.optimization_barrier(tuple(arrived)))
    total = add(*(term for group in terms for term in group))

    head = head.reshape(x_size, -1, channels)
    shares = [pick(head, 0, x_id)]
    for by in (1, -1, 2):
        shares.append(shift(pick(head, 0, (x_id + by) % x_size), "x", by))
    head = add(*shares).astype(BF)
    head = add(head, pair(head, "z", 1)).astype(BF)
    head = add(head, pair(head, "z", 2)).astype(BF)
    head = add(head, pair(head, "z", 4)).astype(BF)
    head = after(head, seconds[0][1])
    pieces = jnp.stack([head] + [shift(head, "x", by) for by in (1, 2, -1)])
    head = jnp.concatenate([pick(pieces, 0, (x_id - x) % x_size) for x in range(x_size)], 0)
    head = after(head.reshape(head_keep.shape), terms[-1][0])
    both = join(head, shift(head, "c", 1), core, 0)
    return total, both.reshape((2 * head_keep.shape[0],) + head_keep.shape[1:])


def local(ecg, conv_first, conv_second, conv_third, enc_gain, ctx_weight, head_weight, sources):
    z_size, x_size, c_size = (lax.axis_size(a) for a in ("z", "x", "c"))
    groups, per_group = sources.shape[1:3]
    z_id, x_id, c_id = (lax.axis_index(a) for a in ("z", "x", "c"))
    owner = sources[0, :, :, 0].reshape(-1)
    block = sources[0, :, :, 1].reshape(-1)
    owner_z = owner // (x_size * c_size)
    owner_x = (owner // c_size) % x_size
    other_core = (owner % c_size != c_id).astype(jnp.int32)
    dx = (owner_x - x_id) % x_size
    dz = (owner_z - z_id) % z_size
    upper = (owner_z >= z_size // 2).astype(jnp.int32)
    bank = jnp.where(
        dx == 0, 0, jnp.where(dx == 3, 1, jnp.where(dx == 1, 2, 3 + upper))
    ) + 5 * other_core
    bank_row = 2 * (owner_z - jnp.where(dx == 2, upper * (z_size // 2), 0)) + block
    position = jnp.where(dz == 0, 7, jnp.where(dz == 4, 0, jnp.where(dz < 4, 7 - 2 * dz, 2 * dz - 8)))
    place = 2 * (dx * z_size + position) + block
    place = place + 2 * x_size * z_size * other_core
    where = jnp.stack([bank, bank_row, place]).astype(jnp.int32)

    target, context = encode(
        ecg.reshape(-1), conv_first, conv_second, conv_third, enc_gain, ctx_weight
    )
    positions, channels = target.shape
    horizon = head_weight.shape[1]
    made = make_queries(target, context, head_weight.transpose(1, 0, 2), groups)
    banks, made = gather_targets(target, made)
    banks = [v.reshape(-1, 128, channels) for v in banks]
    keep, send, pred_grad, pos_terms = score(where, made, banks, horizon, positions, per_group)
    head_keep, head_send, pos_grad = head_product(
        c_id.astype(jnp.int32), context, pred_grad, pos_terms
    )
    shape = (x_size, z_size, positions, channels)
    summed, heads = exchange_back(
        keep.reshape(shape), send.reshape(shape), head_keep, head_send
    )
    target_grad = ((pos_grad + summed) / horizon)[None]
    factor = math.sqrt(channels / (z_size * x_size * c_size * positions))
    head_grad = (heads.astype(F32) * factor).transpose(1, 0, 2)[None]
    return (target_grad, head_grad)


def solution(mesh):
    fine = Mesh(mesh.devices.reshape(8, 4, 2, -1), ("z", "x", "c", "rep"))
    dp = ("z", "x", "c")
    in_specs = (P("rep", dp), P(), P(), P(), P(), P(), P(), P("rep", dp, None, None))
    out_specs = (P("rep", dp, None), P("rep", None, None, None))
    return jax.shard_map(local, mesh=fine, in_specs=in_specs, out_specs=out_specs, check_vma=False)
```

```python
import math

import jax
import jax.numpy as jnp
from jax import lax
from jax.experimental import pallas as pl
from jax.experimental.pallas import tpu as pltpu
from jax.sharding import Mesh, PartitionSpec as P

BF = jnp.bfloat16
F32 = jnp.float32
Z_ORDER = (4, -3, 3, -2, 2, -1, 1, 0)
Z_BUNDLES = (8,)


def gelu_exact(values):
    return jax.nn.gelu(values, approximate=False)


def encode(piece, conv_first, conv_second, conv_third, enc_gain, ctx_weight):
    channels = conv_first.shape[1]
    positions = piece.shape[0] // 20
    frames = piece.reshape(4 * positions, 5)
    hidden_one = gelu_exact(jnp.dot(frames, conv_first, preferred_element_type=F32)).astype(BF)
    hidden_two = gelu_exact(
        jnp.dot(
            hidden_one.reshape(2 * positions, 2 * channels),
            conv_second,
            preferred_element_type=F32,
        )
    ).astype(BF)
    mixed = jnp.dot(
        hidden_two.reshape(positions, 2 * channels), conv_third, preferred_element_type=F32
    )
    average = jnp.mean(mixed, -1, keepdims=True)
    centred = mixed - average
    variance = jnp.mean(centred * centred, -1, keepdims=True)
    latent = (centred / jnp.sqrt(variance + 1e-05) * enc_gain).astype(BF)
    latent_wide = latent.astype(F32)
    target = (
        latent_wide / jnp.sqrt(jnp.sum(latent_wide * latent_wide, -1, keepdims=True) + 1e-06)
    ).astype(BF)
    context = latent
    for layer_index in range(ctx_weight.shape[0]):
        dilation = 2**layer_index
        before = jnp.concatenate(
            [jnp.zeros((dilation, channels), BF), context[: positions - dilation]], 0
        )
        joined = jnp.concatenate([context, before], 1)
        update = gelu_exact(jnp.dot(joined, ctx_weight[layer_index], preferred_element_type=F32))
        context = (context.astype(F32) + update).astype(BF)
    return (target, context)


def query_kernel(tgt_ref, ctx_ref, hw_ref, q_ref, t_ref, stat_ref, pad_s, *, groups):
    positions, channels = tgt_ref.shape
    horizon = hw_ref.shape[0]
    rows = positions // groups
    pad_s[:positions] = tgt_ref[...].astype(F32)
    pad_s[positions:] = jnp.zeros((16, channels), F32)
    position = lax.broadcasted_iota(jnp.int32, (positions, 1), 0)

    unroll = math.gcd(horizon, 3)

    def step(k, ahead):
        pred = jnp.dot(ctx_ref[...], hw_ref[k], preferred_element_type=F32)
        inv = 1.0 / jnp.sqrt(jnp.sum(pred * pred, -1, keepdims=True) + 1e-06)
        query = (pred * inv).astype(BF)
        shifted = pad_s[ahead + 1 : ahead + 1 + positions]
        score = 10.0 * jnp.sum(query.astype(F32) * shifted, -1, keepdims=True)
        usable = jnp.where(position + k + 1 < positions, 10.0, 0.0)
        part = pl.ds(pl.multiple_of(k * rows, rows), rows)
        q_ref[:, part, :] = query.reshape(groups, rows, -1)
        t_ref[:, part, :] = shifted.astype(BF).reshape(groups, rows, -1)
        stat_ref[:, part, 0:1] = inv.reshape(groups, rows, 1)
        stat_ref[:, part, 1:2] = jnp.exp(score).reshape(groups, rows, 1)
        stat_ref[:, part, 2:3] = usable.reshape(groups, rows, 1)

    def steps(i, carry):
        for j in range(unroll):
            step(i * unroll + j, j)
        pad_s[:positions] = pad_s[unroll : unroll + positions]
        return carry

    lax.fori_loop(0, horizon // unroll, steps, 0)


def score_kernel(where_ref, q_ref, t_ref, stat_ref, *rest, per_group, bank_count):
    banks = rest[:bank_count]
    keep_ref, send_ref, pg_ref, p_ref = rest[bank_count : bank_count + 4]
    nbuf, blocks_s, sems, out_sems = rest[bank_count + 4 :]
    batch = q_ref.shape[0]
    horizon = pg_ref.shape[0]
    rows = pg_ref.shape[1] // batch
    entries = nbuf.shape[0]
    at = pl.program_id(0)

    def start(e, carry):
        bank_id = where_ref[0, e]
        row = where_ref[1, e]
        for a in range(bank_count):

            @pl.when(bank_id == a)
            def _():
                pltpu.make_async_copy(banks[a].at[row], nbuf.at[e], sems.at[e]).start()

        return carry

    def arrive(e, carry):
        pltpu.make_async_copy(banks[0].at[0], nbuf.at[e], sems.at[e]).wait()
        return carry

    @pl.when(at == 0)
    def _():
        lax.fori_loop(0, entries, start, 0)
        blocks_s[...] = jnp.zeros(blocks_s.shape, BF)
        lax.fori_loop(0, entries, arrive, 0)

    def weights(j):
        first = (at * batch + j) * per_group
        queries = q_ref[j]
        stat = stat_ref[j]
        pos_exp, ten = stat[:, 1:2], stat[:, 2:3]
        negatives = nbuf[pl.ds(first, per_group)].reshape(per_group * 128, -1)
        negative = lax.dot_general(
            queries, negatives, (((1,), (1,)), ((), ())), preferred_element_type=F32
        )
        neg_exp = jnp.exp2((10.0 * math.log2(math.e)) * negative)
        over = ten / (pos_exp + jnp.sum(neg_exp, -1, keepdims=True))
        weight = (neg_exp * over).astype(BF)
        pos_weight = pos_exp * over - ten
        neg_part = jnp.dot(weight, negatives, preferred_element_type=F32)
        neg_grad = lax.dot_general(
            weight, queries, (((0,), (0,)), ((), ())), preferred_element_type=F32
        )
        return queries, pos_weight, neg_part, neg_grad

    def finish(j, queries, pos_weight, neg_part, neg_grad):
        unit = queries.astype(F32)
        query_grad = pos_weight * t_ref[j].astype(F32) + neg_part
        radial = jnp.sum(unit * query_grad, -1, keepdims=True)
        pred_grad = ((query_grad - unit * radial) * stat_ref[j][:, 0:1]).astype(BF)
        pos_term = (pos_weight * unit).astype(BF)
        for k in range(horizon):
            pg_ref[k, j * rows : (j + 1) * rows, :] = pred_grad[k * rows : (k + 1) * rows]
            p_ref[k, j * rows : (j + 1) * rows, :] = pos_term[k * rows : (k + 1) * rows]
        for s in range(per_group):
            place = where_ref[2, (at * batch + j) * per_group + s]
            block = neg_grad[s * 128 : (s + 1) * 128]
            blocks_s[place] = (blocks_s[place].astype(F32) + block).astype(BF)

    made = [weights(j) for j in range(batch)]
    for j in range(batch):
        finish(j, *made[j])

    @pl.when(at == pl.num_programs(0) - 1)
    def _():
        half = blocks_s.shape[0] // 2
        sent = pltpu.make_async_copy(blocks_s.at[pl.ds(half, half)], send_ref, out_sems.at[0])
        kept = pltpu.make_async_copy(blocks_s.at[pl.ds(0, half)], keep_ref, out_sems.at[1])
        sent.start()
        kept.start()
        sent.wait()
        kept.wait()


def head_kernel(core_ref, ctx_ref, pg_ref, p_ref, hkeep_ref, hsend_ref, pos_ref, pad_s):
    core = core_ref[0]
    half = hkeep_ref.shape[0]

    def head(i, carry):
        for ref, base in ((hkeep_ref, core), (hsend_ref, 1 - core)):
            part = lax.dot_general(
                ctx_ref[...],
                pg_ref[base * half + i],
                (((0,), (0,)), ((), ())),
                preferred_element_type=F32,
            )
            ref[i] = part.astype(BF)
        return carry

    lax.fori_loop(0, half, head, 0)
    positions = pos_ref.shape[0]
    pad_s[...] = jnp.zeros(pad_s.shape, F32)
    for k in range(p_ref.shape[0]):
        at = slice(k + 1, k + 1 + positions)
        pad_s[at] = pad_s[at] + p_ref[k].astype(F32)
    pos_ref[...] = pad_s[:positions]


def make_queries(target, context, head_maps, groups):
    positions, channels = target.shape
    rows = head_maps.shape[0] * positions // groups
    vmem = pl.BlockSpec(memory_space=pltpu.VMEM)
    return pl.pallas_call(
        lambda *refs: query_kernel(*refs, groups=groups),
        out_shape=(
            jax.ShapeDtypeStruct((groups, rows, channels), BF),
            jax.ShapeDtypeStruct((groups, rows, channels), BF),
            jax.ShapeDtypeStruct((groups, rows, 3), F32),
        ),
        in_specs=[vmem] * 3,
        out_specs=(vmem,) * 3,
        scratch_shapes=[pltpu.VMEM((positions + 16, channels), F32)],
        name="queries",
    )(target, context, head_maps)


def score(where, made, banks, horizon, positions, per_group):
    groups, queries, channels = made[0].shape
    blocks = 2 * (positions // 128) * banks[0].shape[0]
    batch = math.gcd(groups, 2)
    span = batch * (positions // groups)
    hbm = pl.BlockSpec(memory_space=pl.ANY)

    def by_group(width):
        return pl.BlockSpec((batch, queries, width), lambda i: (i, 0, 0))

    by_position = pl.BlockSpec((horizon, span, channels), lambda i: (0, i, 0))
    return pl.pallas_call(
        lambda *refs: score_kernel(*refs, per_group=per_group, bank_count=len(banks)),
        grid=(groups // batch,),
        out_shape=(
            jax.ShapeDtypeStruct((blocks, 128, channels), BF),
            jax.ShapeDtypeStruct((blocks, 128, channels), BF),
            jax.ShapeDtypeStruct((horizon, positions, channels), BF),
            jax.ShapeDtypeStruct((horizon, positions, channels), BF),
        ),
        in_specs=[
            pl.BlockSpec(memory_space=pltpu.SMEM),
            by_group(channels),
            by_group(channels),
            by_group(made[2].shape[-1]),
        ]
        + [hbm] * len(banks),
        out_specs=(hbm, hbm, by_position, by_position),
        scratch_shapes=[
            pltpu.VMEM((groups * per_group, 128, channels), BF),
            pltpu.VMEM((2 * blocks, 128, channels), BF),
            pltpu.SemaphoreType.DMA((groups * per_group,)),
            pltpu.SemaphoreType.DMA((2,)),
        ],
        name="score",
    )(where, *made, *banks)


def head_product(core, context, pred_grad, pos_terms):
    horizon, positions, channels = pred_grad.shape
    vmem = pl.BlockSpec(memory_space=pltpu.VMEM)
    half = jax.ShapeDtypeStruct((horizon // 2, channels, channels), BF)
    return pl.pallas_call(
        head_kernel,
        out_shape=(half, half, jax.ShapeDtypeStruct((positions, channels), F32)),
        in_specs=[pl.BlockSpec(memory_space=pltpu.SMEM), vmem, vmem, vmem],
        out_specs=(vmem, vmem, vmem),
        scratch_shapes=[pltpu.VMEM((positions + 16, channels), F32)],
        name="heads",
    )(core.reshape(1), context, pred_grad, pos_terms)


def shift(values, axis, by):
    size = lax.axis_size(axis)
    return lax.ppermute(values, axis, [(i, (i + by) % size) for i in range(size)])


def exchange(values, axis):
    return lax.all_to_all(values, axis, 0, 0, tiled=True)


def add(*terms):
    total = terms[0].astype(F32)
    for term in terms[1:]:
        total = total + term.astype(F32)
    return total


def gather_targets(target, made):
    z_size = lax.axis_size("z")
    row = exchange(jnp.broadcast_to(target[None], (z_size,) + target.shape), "z")
    left = shift(row, "x", 1)
    right = shift(row, "x", -1)
    left, right, *made = lax.optimization_barrier((left, right, *made))
    far_low = shift(left[: z_size // 2], "x", 1)
    far_high = shift(right[z_size // 2 :], "x", -1)
    mine = [row, left, right, far_low, far_high]
    return mine + [shift(v, "c", 1) for v in mine], made


def pair(values, axis, bit):
    size = lax.axis_size(axis)
    return lax.ppermute(values, axis, [(i, i ^ bit) for i in range(size)])


def pick(values, axis, at):
    return lax.dynamic_index_in_dim(values, at, axis, keepdims=False)


def join(mine, other, bit, axis):
    low = jnp.where(bit == 0, mine, other)
    high = jnp.where(bit == 0, other, mine)
    return jnp.stack([low, high], axis)


def after(values, other):
    zero = other[(0,) * (other.ndim - 1) + (slice(0, 1),)].astype(F32) * 0.0
    return (values.astype(F32) + zero.reshape(())).astype(values.dtype)


def exchange_back(keep, send, head_keep, head_send):
    x_id, core = lax.axis_index("x"), lax.axis_index("c")
    x_size, channels = lax.axis_size("x"), keep.shape[-1]
    received = shift(send, "c", 1)
    head = add(head_keep, shift(head_send, "c", 1)).astype(BF)
    starts = [sum(Z_BUNDLES[:i]) for i in range(len(Z_BUNDLES))]

    firsts, seconds, terms = [], [], []
    for first, count in zip(starts, Z_BUNDLES):
        span = slice(first, first + count)
        far_low = add(keep[2, span, :128], received[2, span, :128]).astype(BF)
        far_high = add(keep[2, span, 128:], received[2, span, 128:]).astype(BF)
        firsts.append([shift(far_low, "x", 1), shift(far_high, "x", -1)])
    for i, (first, count) in enumerate(zip(starts, Z_BUNDLES)):
        span = slice(first, first + count)
        low, high, keep, received = lax.optimization_barrier((*firsts[i], keep, received))
        rest = keep.shape[2] - 128
        low = jnp.pad(low, ((0, 0), (0, rest), (0, 0)))
        high = jnp.pad(high, ((0, 0), (rest, 0), (0, 0)))
        ahead = add(keep[1, span], received[1, span], low).astype(BF)
        behind = add(keep[3, span], received[3, span], high).astype(BF)
        seconds.append([shift(ahead, "x", 1), shift(behind, "x", -1)])
    for i, (first, count) in enumerate(zip(starts, Z_BUNDLES)):
        span = slice(first, first + count)
        sums = add(keep[0, span], received[0, span], *seconds[i])
        arrived = []
        for j in range(count):
            by = Z_ORDER[first + j]
            arrived.append(sums[j] if by == 0 else shift(sums[j].astype(BF), "z", by))
        terms.append(lax.optimization_barrier(tuple(arrived)))
    total = add(*(term for group in terms for term in group))

    head = head.reshape(x_size, -1, channels)
    shares = [pick(head, 0, x_id)]
    for by in (1, -1, 2):
        shares.append(shift(pick(head, 0, (x_id + by) % x_size), "x", by))
    head = add(*shares).astype(BF)
    head = add(head, pair(head, "z", 1)).astype(BF)
    head = add(head, pair(head, "z", 2)).astype(BF)
    head = add(head, pair(head, "z", 4)).astype(BF)
    head = after(head, seconds[0][1])
    pieces = jnp.stack([head] + [shift(head, "x", by) for by in (1, 2, -1)])
    head = jnp.concatenate([pick(pieces, 0, (x_id - x) % x_size) for x in range(x_size)], 0)
    head = after(head.reshape(head_keep.shape), terms[-1][0])
    both = join(head, shift(head, "c", 1), core, 0)
    return total, both.reshape((2 * head_keep.shape[0],) + head_keep.shape[1:])


def local(ecg, conv_first, conv_second, conv_third, enc_gain, ctx_weight, head_weight, sources):
    z_size, x_size, c_size = (lax.axis_size(a) for a in ("z", "x", "c"))
    groups, per_group = sources.shape[1:3]
    z_id, x_id, c_id = (lax.axis_index(a) for a in ("z", "x", "c"))
    owner = sources[0, :, :, 0].reshape(-1)
    block = sources[0, :, :, 1].reshape(-1)
    owner_z = owner // (x_size * c_size)
    owner_x = (owner // c_size) % x_size
    other_core = (owner % c_size != c_id).astype(jnp.int32)
    dx = (owner_x - x_id) % x_size
    dz = (owner_z - z_id) % z_size
    upper = (owner_z >= z_size // 2).astype(jnp.int32)
    bank = jnp.where(
        dx == 0, 0, jnp.where(dx == 3, 1, jnp.where(dx == 1, 2, 3 + upper))
    ) + 5 * other_core
    bank_row = 2 * (owner_z - jnp.where(dx == 2, upper * (z_size // 2), 0)) + block
    position = jnp.where(dz == 0, 7, jnp.where(dz == 4, 0, jnp.where(dz < 4, 8 - 2 * dz, 2 * dz - 9)))
    place = 2 * (dx * z_size + position) + block
    place = place + 2 * x_size * z_size * other_core
    where = jnp.stack([bank, bank_row, place]).astype(jnp.int32)

    target, context = encode(
        ecg.reshape(-1), conv_first, conv_second, conv_third, enc_gain, ctx_weight
    )
    positions, channels = target.shape
    horizon = head_weight.shape[1]
    made = make_queries(target, context, head_weight.transpose(1, 0, 2), groups)
    banks, made = gather_targets(target, made)
    banks = [v.reshape(-1, 128, channels) for v in banks]
    keep, send, pred_grad, pos_terms = score(where, made, banks, horizon, positions, per_group)
    head_keep, head_send, pos_grad = head_product(
        c_id.astype(jnp.int32), context, pred_grad, pos_terms
    )
    shape = (x_size, z_size, positions, channels)
    summed, heads = exchange_back(
        keep.reshape(shape), send.reshape(shape), head_keep, head_send
    )
    target_grad = ((pos_grad + summed) / horizon)[None]
    factor = math.sqrt(channels / (z_size * x_size * c_size * positions))
    head_grad = (heads.astype(F32) * factor).transpose(1, 0, 2)[None]
    return (target_grad, head_grad)


def solution(mesh):
    fine = Mesh(mesh.devices.reshape(8, 4, 2, -1), ("z", "x", "c", "rep"))
    dp = ("z", "x", "c")
    in_specs = (P("rep", dp), P(), P(), P(), P(), P(), P(), P("rep", dp, None, None))
    out_specs = (P("rep", dp, None), P("rep", None, None, None))
    return jax.shard_map(local, mesh=fine, in_specs=in_specs, out_specs=out_specs, check_vma=False)
```
